32 devices in a mesh: group: 2 (over y), seq: 4 (over z), head: 2 (over x), cfg: 2 (over core).
Axes of the slice: x: 2, y: 2, z: 4, core: 2. Of those that a mesh axis runs over, the one named last changes fastest.
Arguments:
- residual: bfloat16 [2, 1024, 3072], P('cfg', ('group', 'seq', 'head')), parts along dimension 1, may hold values from -56 to 56
- queries: bfloat16 [2, 1024, 1536], P('cfg', ('group', 'seq', 'head')), parts along dimension 1, may hold values from -8 to 8
- key_rows: bfloat16 [2, 1024, 1536], P('cfg', ('group', 'seq', 'head')), parts along dimension 1, may hold values from -8 to 8
- value_rows: bfloat16 [2, 1024, 1536], P('cfg', ('group', 'seq', 'head')), parts along dimension 1, may hold values from -6 to 6
- out_weight: bfloat16 [1536, 3072], P('head'), may hold values from -0.15625 to 0.15625
- modulation: float32 [2, 8, 3072], P('cfg', 'group'), parts along dimension 1, may hold values from -1 to 1
- router: bfloat16 [3072, 8], replicated, may hold values from -0.109375 to 0.109375
- gate_weight: bfloat16 [8, 3072, 1024], P(('seq', 'cfg'), None, 'head'), may hold values from -0.109375 to 0.109375
- up_weight: bfloat16 [8, 3072, 1024], P(('seq', 'cfg'), None, 'head'), may hold values from -0.109375 to 0.109375
- down_weight: bfloat16 [8, 1024, 3072], P(('seq', 'cfg'), 'head'), may hold values from -0.1875 to 0.1875
- expert_ids: int32 [2, 1024, 2], P('cfg', ('group', 'seq', 'head')), parts along dimension 1, may hold values from 0 to 7, all different within a row; in each aligned block of 64 rows (0 to 63, 64 to 127, ..., all dimensions but the last counted through in order) at most 20 rows name the same one
Outputs:
- updated: bfloat16 [2, 1024, 3072], P('cfg', ('group', 'seq', 'head')), parts along dimension 1
The draws below stay inside these ranges and needn't reach their ends.
There are 2 independent parts, one for each index of `group`. The reference program is written for one: setup_inputs(seed, part) draws one part's arguments, and reference() takes and returns one part's arrays. A program takes and returns all parts, laid end to end along the dimension named above; an argument that names none is the same for every part. Nothing has to cross between parts.
Inputs may be any that keep to these rules, and one draw needn't show every extreme that they name: `expert_ids`: each row names 2 different experts. In each aligned block of 64 rows (branch and position taken in order, the rows of one device) no expert is named by more than 20 rows.
All inputs are finite; a program needn't handle non-finite values.
Results may differ from the reference program's by a relative error of at most 0.008.
Values may be sent and summed in bfloat16 or wider, within the bound.
A program may use at most 64 MiB of HBM per device.

```python
import math
import jax
import jax.numpy as jnp
import numpy as np
from jax import lax

D = 3072
HEADS = 12
HEAD_DIM = 128
FF = 1024
TOP = 2
TOK_DEV = 64
HF = 1536
L = 512
EXPERTS = 8
CAP = 20
N_HEAD = 2


def common_keys(key):
    return jnp.clip(jax.random.normal(jax.random.fold_in(key, 13), (2, L, HF), jnp.float32), -6.0, 6.0)


def drawn_queries(key):
    key_values = common_keys(key).reshape(2, L, HEADS, HEAD_DIM)
    base = jax.random.fold_in(key, 7101)
    partner = jax.random.randint(jax.random.fold_in(base, 1), (2, L, HEADS), 0, L)
    strength = jax.random.uniform(jax.random.fold_in(base, 2), (2, L, HEADS, 1), jnp.float32, 0.6, 1.6)
    noise = jnp.clip(jax.random.normal(jax.random.fold_in(base, 3), (2, L, HEADS, HEAD_DIM), jnp.float32), -6.0, 6.0)
    branch_index = jnp.arange(2, dtype=jnp.int32)[:, None, None]
    head_index = jnp.arange(HEADS, dtype=jnp.int32)[None, None, :]
    target = key_values[branch_index, partner, head_index]
    values = jnp.clip(strength * target + noise, -8.0, 8.0)
    return values.reshape(2, L, HF)


def draw_queries(key, part):
    values = drawn_queries(key)
    return values.astype(jnp.bfloat16)


def draw_key_rows(key, part):
    values = common_keys(key)
    return values.astype(jnp.bfloat16)


def draw_residual(key, part):
    values = jnp.clip(jax.random.normal(jax.random.fold_in(key, 21), (2, L, D), jnp.float32), -5.0, 5.0)
    return values.astype(jnp.bfloat16)


def block_scale(rng, dims, shards, low, largest):
    level, own = 1.0, jax.random.fold_in(rng, 6)
    for dim, parts in shards:
        steps = jnp.exp(jax.random.uniform(jax.random.fold_in(own, dim), (parts,), jnp.float32, low / len(shards), largest / len(shards)))
        level = level * jnp.repeat(steps, dims[dim] // parts).reshape([-1 if axis == dim else 1 for axis in range(len(dims))])
    return level


def assign_block(stream_key, own, number, rows, count, top, limit, slope):
    sequence = jax.random.permutation(stream_key, count)
    crowded, common = portions_of(count, rows * top, limit, slope, True), portions_of(count, rows * top, limit, slope, False)
    places = jnp.arange(count)

    def named(lengths, turn):
        used = int((lengths > 0).sum())
        fixed = max(1, used // 4)
        passed = fixed + (places - fixed + turn * (used - fixed)) % max(1, count - fixed)
        return jnp.zeros((count,), jnp.int32).at[sequence[jnp.where(places < fixed, places, passed)]].set(jnp.asarray(lengths, jnp.int32))

    lengths = jnp.where(number % 4 == 0, named(crowded, number // 4), named(common, number - number // 4 - 1))
    mixed = jax.random.permutation(jax.random.fold_in(own, 3), count)
    giver, sink = mixed[0:count // 2 * 2:2], mixed[1:count // 2 * 2:2]
    room = jnp.minimum(lengths[giver] - 1, limit - lengths[sink]) // 2
    room = jnp.where((giver == sequence[0]) | (sink == sequence[0]) | (lengths[sink] == 0), 0, jnp.maximum(room, 0))
    passed = jax.random.randint(jax.random.fold_in(own, 4), (count // 2,), 0, 1 << 20) % (room + 1)
    lengths = lengths.at[giver].add(-passed).at[sink].add(passed)
    members = jnp.searchsorted(jnp.cumsum(lengths), jnp.arange(rows * top), side="right").astype(jnp.int32)
    table = members.reshape(top, rows).T
    table = table[jax.random.permutation(jax.random.fold_in(own, 1), rows)]
    turn = jax.random.randint(jax.random.fold_in(own, 2), (rows, 1), 0, top)
    return jnp.take_along_axis(table, (jnp.arange(top)[None, :] + turn) % top, axis=1)


def portions_of(number_of, total, reach, skew, full):
    portions = [(1 << 20) // math.isqrt(rank ** skew) + 1 for rank in range(1, number_of + 1)]
    largest = reach if full else min(reach, max(-(-total // number_of), total * portions[0] // sum(portions)))
    least = 1 if total - largest >= number_of - 1 else 0
    given, spare = [largest] + [least] * (number_of - 1), total - largest - least * (number_of - 1)
    while spare > 0:
        movable = [i for i in range(1, number_of) if given[i] < largest] or [i for i in range(1, number_of) if given[i] < reach]
        whole, remaining = sum([portions[i] for i in movable]), spare
        for i in movable:
            extra = min(reach - given[i], max(1, remaining * portions[i] // whole), spare)
            given[i] = given[i] + extra
            spare = spare - extra
    return np.array(given)


def gaussian(stream_key, shape, deviation, limit, split=(), kind=jnp.bfloat16):
    values = jax.random.normal(stream_key, shape, jnp.float32) * deviation
    if len(split) > 0:
        values = block_scale(stream_key, shape, split, -0.22, 0.18) * values
    return jnp.clip(values, min=-limit, max=limit).astype(kind)


def setup_inputs(seed: int = 0, part: int = 0) -> dict:
    streams_of = jax.random.split(jax.random.key(seed), 12)
    part_splits = jax.random.split(jax.random.fold_in(streams_of[11], part), 12)
    residual = draw_residual(jax.random.fold_in(jax.random.fold_in(streams_of[11], part), 71), part)
    queries = draw_queries(jax.random.fold_in(jax.random.fold_in(streams_of[11], part), 71), part)
    key_rows = draw_key_rows(jax.random.fold_in(jax.random.fold_in(streams_of[11], part), 71), part)
    value_rows = gaussian(part_splits[3], (2, L, HF), 1.0, 6.0, ((0, 2), (1, 8)))
    out_weight = gaussian(streams_of[4], (HF, D), HF ** -0.5, 0.15625, ((0, 2),))
    modulation = jnp.clip(jax.random.uniform(part_splits[5], (2, 4, D), jnp.float32, -1.0, 1.0) * block_scale(part_splits[5], (2, 4, D), ((0, 2),), -0.4, 0.0), -1.0, 1.0)
    router = gaussian(streams_of[6], (D, EXPERTS), D ** -0.5, 0.109375)
    gate_weight = gaussian(streams_of[7], (EXPERTS, D, FF), D ** -0.5, 0.109375, ((0, 8), (2, 2)))
    up_weight = gaussian(streams_of[8], (EXPERTS, D, FF), D ** -0.5, 0.109375, ((0, 8), (2, 2)))
    down_weight = gaussian(streams_of[9], (EXPERTS, FF, D), FF ** -0.5, 0.1875, ((0, 8), (1, 2)))
    expert_ids_keys = jax.random.split(jax.random.fold_in(part_splits[10], 1), 2 * L // TOK_DEV)
    expert_ids_turns = jax.random.permutation(jax.random.fold_in(part_splits[10], 3), 2 * L // TOK_DEV)
    expert_ids = jax.vmap(lambda own, number: assign_block(jax.random.fold_in(part_splits[10], 2), own, number, TOK_DEV, EXPERTS, TOP, CAP, 2))(expert_ids_keys, expert_ids_turns).reshape((2, L, TOP))
    return {"residual": residual, "queries": queries, "key_rows": key_rows, "value_rows": value_rows, "out_weight": out_weight, "modulation": modulation, "router": router, "gate_weight": gate_weight, "up_weight": up_weight, "down_weight": down_weight, "expert_ids": expert_ids}


EPSILON = 1e-06

def attend_head(operands):
    query_rows, key_block, value_block = operands
    scores = jnp.dot(query_rows, key_block.T, preferred_element_type=jnp.float32) * (1.0 / math.sqrt(HEAD_DIM))
    highest = lax.optimization_barrier(jnp.max(scores, axis=1, keepdims=True))
    weights = jnp.exp(scores - highest)
    totals = lax.optimization_barrier(jnp.sum(weights, axis=1, keepdims=True))
    numerator = jnp.dot(weights.astype(jnp.bfloat16), value_block, preferred_element_type=jnp.float32)
    return (numerator / totals).astype(jnp.bfloat16)

def split_heads(stacked):
    return stacked.reshape(2, L, HEADS, HEAD_DIM).transpose(0, 2, 1, 3).reshape(2 * HEADS, L, HEAD_DIM)

def blocked_sum(left_side, right_side, blocks):
    block_width = left_side.shape[1] // blocks
    running = None
    for position in range(blocks):
        partial_sum = jnp.dot(left_side[:, position * block_width:(position + 1) * block_width], right_side[position * block_width:(position + 1) * block_width], preferred_element_type=jnp.float32)
        partial_sum = lax.optimization_barrier(partial_sum.astype(jnp.bfloat16)).astype(jnp.float32)
        running = partial_sum if running is None else running + partial_sum
    return running

def expert_apply(operands):
    row_block, gate_part, up_part, down_part = operands
    gate_out = jnp.dot(row_block, gate_part, preferred_element_type=jnp.float32)
    up_out = jnp.dot(row_block, up_part, preferred_element_type=jnp.float32)
    activated = (jax.nn.silu(gate_out) * up_out).astype(jnp.bfloat16)
    return blocked_sum(activated, down_part, N_HEAD).astype(jnp.bfloat16)

def reference(residual, queries, key_rows, value_rows, out_weight, modulation, router, gate_weight, up_weight, down_weight, expert_ids):
    attended = lax.map(attend_head, (split_heads(queries), split_heads(key_rows), split_heads(value_rows)))
    attended = attended.reshape(2, HEADS, L, HEAD_DIM).transpose(0, 2, 1, 3).reshape(2 * L, HF)
    projected = blocked_sum(attended, out_weight, N_HEAD).reshape(2, L, D)
    hidden = residual.astype(jnp.float32) + modulation[:, 0][:, None, :] * projected
    average = lax.optimization_barrier(jnp.mean(hidden, axis=-1, keepdims=True))
    centered = hidden - average
    variance = lax.optimization_barrier(jnp.mean(centered * centered, axis=-1, keepdims=True))
    normed = centered * lax.rsqrt(variance + EPSILON)
    mixed_in = (normed * (1.0 + modulation[:, 2][:, None, :]) + modulation[:, 1][:, None, :]).astype(jnp.bfloat16)
    mixed_in = mixed_in.reshape(2 * L, D)
    logits = jnp.dot(mixed_in, router, preferred_element_type=jnp.float32)
    flat_ids = expert_ids.reshape(2 * L, TOP).astype(jnp.int32)
    chosen = jnp.take_along_axis(logits, flat_ids, axis=1)
    gate_values = jnp.stack([jax.nn.sigmoid(chosen[:, 0] - chosen[:, 1]), jax.nn.sigmoid(chosen[:, 1] - chosen[:, 0])], axis=1)
    blocks = 2 * L // TOK_DEV
    onehot = (flat_ids.reshape(blocks, TOK_DEV * TOP)[:, :, None] == jnp.arange(EXPERTS, dtype=jnp.int32)).astype(jnp.int32)
    earlier = jnp.cumsum(onehot, axis=1) - onehot
    slot_index = lax.optimization_barrier(jnp.sum(earlier * onehot, axis=2)).reshape(2 * L, TOP).astype(jnp.int32)
    block_index = ((jnp.arange(2 * L, dtype=jnp.int32) // TOK_DEV)[:, None] * jnp.ones((1, TOP), jnp.int32)).astype(jnp.int32)
    source = jnp.broadcast_to(mixed_in[:, None, :], (2 * L, TOP, D))
    buffer = jnp.zeros((EXPERTS, blocks, CAP, D), jnp.bfloat16)
    buffer = buffer.at[flat_ids, block_index, slot_index].set(source)
    processed = lax.map(expert_apply, (buffer.reshape(EXPERTS, blocks * CAP, D), gate_weight, up_weight, down_weight))
    processed = processed.reshape(EXPERTS, blocks, CAP, D)
    picked = processed[flat_ids, block_index, slot_index].astype(jnp.float32)
    expert_mix = lax.optimization_barrier(jnp.sum(gate_values[:, :, None] * picked, axis=1)).reshape(2, L, D)
    return (hidden + modulation[:, 3][:, None, :] * expert_mix).astype(jnp.bfloat16)
```

```python
import functools
import jax
import jax.numpy as jnp
import numpy as np
from jax import lax
from jax.experimental import pallas as pl
from jax.experimental.pallas import tpu as pltpu
from jax.sharding import PartitionSpec as P

HEAD_DIM = 128
EPSILON = 1e-06
QUARTERS = 4
MESH = pl.DeviceIdType.MESH
F32 = jnp.float32
BF16 = jnp.bfloat16


def order(groups, size):
    def every(step, n):
        return [(step, n, d) for d in range(size)]

    if groups == 1:
        return every("F", 0) + [("D", 0, 0)] + every("Y", 0) + every("Z", 0)
    if groups == 2:
        return (
            every("F", 0) + [("D", 0, 0)] + every("F", 1) + every("Y", 0) + [("D", 1, 0)]
            + every("Y", 1) + every("Z", 1) + every("Z", 0)
        )
    if size != 2:
        steps = every("F", 0) + every("F", 1) + every("F", 2) + every("F", 3)
        for n in (1, 2, 3, 0):
            steps += [("D", n, 0)] + every("Y", n)
        return steps + every("Z", 1) + every("Z", 2) + every("Z", 3) + every("Z", 0)
    return [
        ("F", 0, 1), ("F", 1, 0), ("F", 1, 1), ("F", 2, 0), ("F", 2, 1), ("D", 1, 0), ("Y", 1, 0),
        ("F", 3, 0), ("F", 0, 0), ("D", 2, 0), ("Z", 1, 0), ("F", 3, 1), ("Y", 1, 1), ("D", 0, 0),
        ("Y", 2, 0), ("D", 3, 0), ("Z", 1, 1), ("Y", 3, 0), ("Y", 2, 1), ("Y", 3, 1), ("Y", 0, 1),
        ("Z", 2, 0), ("Z", 3, 0), ("Z", 2, 1), ("Y", 0, 0), ("Z", 3, 1), ("Z", 0, 1), ("Z", 0, 0),
    ]


def kernel(
    sizes,
    q_hbm, k_hbm, v_hbm, wo_hbm, wg_hbm, wu_hbm, wd_hbm, *rest
):
    S, H, C, T, F, D, E, A, B, R, parts, groups = sizes
    small = 12
    small_hbm, out_ref, rest = rest[:small], rest[small], rest[small + 1 :]
    small_ref, rest = rest[:small], rest[small:]
    (res_ref, mod_ref, router_ref, ids_ref, tile_ref, tile_t_ref,
     upper_ref, lower_ref, rowkey_ref, rowkey_t_ref, perm_ref, perm_t_ref) = small_ref
    P2 = len(parts)
    kbufs, rest = rest[:P2], rest[P2:]
    vbufs, rest = rest[:P2], rest[P2:]
    qbufs, rest = rest[:P2], rest[P2:]
    atts, rest = rest[:P2], rest[P2:]
    (hand, wo, wg, wu, wd,
     pbuf, prec, hidden, mixq,
     xout, xin, xs, yout, yrec, ysum, ret, placing, picks,
     ssem, lsem, wsem, kv_recv, kv_xsend, kv_zsend, q_send, q_recv, h_send, h_recv, a_send, a_recv,
     p_send, p_recv, d_send, d_recv, dx_send, y_send, y_recv, r_send, r_recv) = rest
    N = S * C
    W = D // QUARTERS
    z, x, c = lax.axis_index("seq"), lax.axis_index("head"), lax.axis_index("cfg")
    me = z * C + c
    handing = any(p[2] for p in parts)

    small_loads = [pltpu.make_async_copy(a, b, ssem.at[i]) for i, (a, b) in enumerate(zip(small_hbm, small_ref))]
    for load in small_loads:
        load.start()

    def partner(d):
        return lax.rem(x + d, H)

    half = S // 2

    def near(n):
        if S % 2:
            return lax.rem(z + n, S)
        side = lax.rem(z // half + n % 2, 2)
        return side * half + lax.rem(lax.rem(z, half) + n // 2, half)

    def other(d):
        to_z, to_c = near(d // C), lax.rem(c + d % C, C)
        return to_z * C + to_c, {"seq": to_z, "cfg": to_c}

    def origin(d):
        return near(d // C) * C + lax.rem(c - d % C + C, C)

    def rows(i):
        return pl.ds(pl.multiple_of(i * T, T), T)

    def remote(src, dst, send, recv, device):
        return pltpu.make_async_remote_copy(
            src_ref=src, dst_ref=dst, send_sem=send, recv_sem=recv,
            device_id=device, device_id_type=MESH,
        )

    barrier = pltpu.get_barrier_semaphore()

    def greet(device):
        pl.semaphore_signal(barrier, inc=1, device_id=device, device_id_type=MESH)

    for d in range(1, H):
        greet({"head": partner(d)})
    for d in range(1, C):
        greet({"cfg": lax.rem(c + d, C)})
    for d in range(H):
        @pl.when(z < S - 1)
        def _():
            greet({"seq": z + 1, "head": partner(d)})

        @pl.when(z > 0)
        def _():
            greet({"seq": z - 1, "head": partner(d)})

    sides = jnp.where(z < S - 1, 1, 0) + jnp.where(z > 0, 1, 0)
    pl.semaphore_wait(barrier, H - 1 + C - 1 + H * sides)

    kv_src, kv_buf = (k_hbm, v_hbm), (kbufs, vbufs)
    outer = (z == 0) | (z == S - 1)
    inner = jnp.logical_not(outer)
    helping = (z == 1) | (z == S - 2)
    helper = jnp.where(z == 0, 1, S - 2)
    helped = jnp.where(z == 1, 0, S - 1)

    def cols(part, p):
        first, count, _ = parts[part]
        return pl.ds(pl.multiple_of(p * F + first * HEAD_DIM, 128), count * HEAD_DIM)

    def x_copy(kv, part, d):
        p = partner(d)
        return remote(
            kv_src[kv].at[:, cols(part, p)], kv_buf[kv][part].at[rows(x * S + z)],
            kv_xsend.at[kv, part, d - 1], kv_recv.at[kv, part, x * S + z], {"head": p},
        )

    def own_copy(kv, part):
        return pltpu.make_async_copy(
            kv_src[kv].at[:, cols(part, x)], kv_buf[kv][part].at[rows(x * S + z)], lsem.at[kv, part]
        )

    def z_copy(kv, part, ox, oz, step, own):
        block = ox * S + oz
        src = kv_src[kv].at[:, cols(part, x)] if own else kv_buf[kv][part].at[rows(block)]
        return remote(
            src, kv_buf[kv][part].at[rows(block)],
            kv_zsend.at[kv, part, block, 0 if step > 0 else 1], kv_recv.at[kv, part, block],
            {"seq": z + step},
        )

    def right(part):
        return z + 1 <= (S - 2 if parts[part][2] else S - 1)

    def leftward(part):
        return z - 1 >= (1 if parts[part][2] else 0)

    def both_ways(kv, part, ox, own, act):
        @pl.when(right(part))
        def _():
            act(z_copy(kv, part, ox, z, 1, own))

        @pl.when(leftward(part))
        def _():
            act(z_copy(kv, part, ox, z, -1, own))

    def q_copy(part, d):
        p = partner(d)
        return remote(
            q_hbm.at[:, cols(part, p)], qbufs[part].at[rows(x)],
            q_send.at[part, d - 1], q_recv.at[part, x], {"head": p},
        )

    def own_q(part):
        return pltpu.make_async_copy(q_hbm.at[:, cols(part, x)], qbufs[part].at[rows(x)], lsem.at[2, part])

    def hand_copy(d):
        p = partner(d)
        return remote(
            q_hbm.at[:, cols(0, p)], hand.at[rows(x)],
            h_send.at[d], h_recv.at[x], {"seq": helper, "head": p},
        )

    def give_back():
        return remote(hand, atts[0], a_send.at[0], a_recv.at[0], {"seq": helped})

    def q_start(part):
        if parts[part][2]:
            @pl.when(inner)
            def _():
                for d in range(1, H):
                    q_copy(part, d).start()
                own_q(part).start()

            @pl.when(outer)
            def _():
                for d in range(H):
                    hand_copy(d).start()
        else:
            for d in range(1, H):
                q_copy(part, d).start()
            own_q(part).start()

    def q_wait(part):
        own_q(part).wait()
        for d in range(1, H):
            p = partner(d)
            pltpu.make_async_copy(
                qbufs[part].at[rows(p)], qbufs[part].at[rows(p)], q_recv.at[part, p]
            ).wait()

    def begin(part):
        for kv in range(2):
            for d in range(1, H):
                x_copy(kv, part, d).start()
            both_ways(kv, part, x, True, lambda copy: copy.start())

    for part in range(P2):
        begin(part)
    for part in range(P2):
        q_start(part)
    for part in range(P2):
        for kv in range(2):
            own_copy(kv, part).start()
    loads = [
        pltpu.make_async_copy(a, b, wsem.at[i])
        for i, (a, b) in enumerate(((wo_hbm, wo), (wg_hbm.at[0], wg), (wu_hbm.at[0], wu), (wd_hbm.at[0], wd)))
    ]
    for load in loads:
        load.start()

    def arrived(kv, part, block):
        pltpu.make_async_copy(
            kv_buf[kv][part].at[rows(block)], kv_buf[kv][part].at[rows(block)], kv_recv.at[kv, part, block]
        ).wait()

    def relay(kv, part, j):
        if j == 0:
            for d in range(1, H):
                ox = partner(d)
                arrived(kv, part, ox * S + z)
                both_ways(kv, part, ox, False, lambda copy: copy.start())
            return
        low, high = (1, S - 2) if parts[part][2] else (0, S - 1)
        for d in range(H):
            ox = partner(d)

            @pl.when((z - j >= 0) & (z <= high))
            def _():
                arrived(kv, part, ox * S + z - j)

                @pl.when(z + 1 <= high)
                def _():
                    z_copy(kv, part, ox, z - j, 1, False).start()

            @pl.when((z + j < S) & (z >= low))
            def _():
                arrived(kv, part, ox * S + z + j)

                @pl.when(z - 1 >= low)
                def _():
                    z_copy(kv, part, ox, z + j, -1, False).start()

    for load in small_loads[3:10]:
        load.wait()
    ids = ids_ref[...].astype(F32).astype(BF16)
    ids_row = jnp.dot(ids, tile_ref[...], preferred_element_type=F32)
    ids_col = lax.dot_general(tile_t_ref[...], ids, (((1,), (1,)), ((), ())), preferred_element_type=F32)
    expert_rows = lax.broadcasted_iota(jnp.int32, (E, QUARTERS * T), 0).astype(F32)
    hot_row = [(ids_row[k : k + 1, :] == expert_rows).astype(F32) for k in range(2)]
    named = (hot_row[0] + hot_row[1])[:, :T].astype(BF16)
    earlier = jnp.dot(named, upper_ref[...], preferred_element_type=F32)
    slots = A + B
    quarter_row = (lax.broadcasted_iota(jnp.int32, (1, QUARTERS * T), 1) // T * (E * slots)).astype(F32)
    key_row = [
        quarter_row
        + ids_row[k : k + 1, :] * slots
        + jnp.sum(earlier * hot_row[k], axis=0, keepdims=True)
        for k in range(2)
    ]
    expert_cols = lax.broadcasted_iota(jnp.int32, (QUARTERS * T, E), 1).astype(F32)
    hot_col = [(ids_col[:, k : k + 1] == expert_cols).astype(F32) for k in range(2)]
    named = (hot_col[0] + hot_col[1])[:T, :].astype(BF16)
    earlier = jnp.dot(lower_ref[...], named, preferred_element_type=F32)
    quarter_col = (lax.broadcasted_iota(jnp.int32, (QUARTERS * T, 1), 0) // T * (E * slots)).astype(F32)
    key_col = [
        quarter_col
        + ids_col[:, k : k + 1] * slots
        + jnp.sum(earlier * hot_col[k], axis=1, keepdims=True)
        for k in range(2)
    ]

    placing[...] = (
        (rowkey_ref[...] == key_row[0]).astype(F32) + (rowkey_ref[...] == key_row[1]).astype(F32)
    ).astype(BF16)
    for k in range(2):
        picks[k] = (key_col[k] == rowkey_t_ref[...]).astype(BF16)

    heads = F // HEAD_DIM
    block_rows = H * T if H * T * H * S * T <= 131072 else T
    blocks = H * T // block_rows
    factor = HEAD_DIM ** (-0.5)

    def over_blocks(body):
        if blocks == 1:
            body(slice(0, block_rows))
        else:
            def step(i, carry):
                body(pl.ds(pl.multiple_of(i * block_rows, block_rows), block_rows))
                return carry

            lax.fori_loop(0, blocks, step, 0)


    def score(part, q, r, h):
        span = slice(h * HEAD_DIM, (h + 1) * HEAD_DIM)
        s = lax.dot_general(
            q[r, span], kbufs[part][:, span], (((1,), (1,)), ((), ())), preferred_element_type=F32,
        ) * factor
        w = jnp.exp(s - jnp.max(s, axis=1, keepdims=True))
        return w.astype(BF16), jnp.sum(w, axis=1, keepdims=True)

    def attend(part, q, out):
        for h in range(parts[part][1]):
            span = slice(h * HEAD_DIM, (h + 1) * HEAD_DIM)

            def body(r):
                w, total = score(part, q, r, h)
                u = jnp.dot(w, vbufs[part][:, span], preferred_element_type=F32)
                out[r, span] = (u / total).astype(BF16)

            over_blocks(body)

    def early():
        own_copy(0, 0).wait()
        own_copy(1, 0).wait()
        if parts[0][2]:
            @pl.when(helping)
            def _():
                for d in range(H):
                    p = partner(d)
                    pltpu.make_async_copy(hand.at[rows(p)], hand.at[rows(p)], h_recv.at[p]).wait()
                attend(0, hand, hand)
                give_back().start()

            @pl.when(inner)
            def _():
                q_wait(0)
                attend(0, qbufs[0], atts[0])
        else:
            q_wait(0)
            attend(0, qbufs[0], atts[0])

    def step(j, among):
        for part in among:
            for kv in range(2):
                relay(kv, part, j)

    middle = S // 2 if P2 > 1 else S - 1
    for j in range(middle + 1):
        step(j, range(P2))
    for j in range(middle + 1, S):
        step(j, range(1))
    early()
    for part in range(1, P2):
        for j in range(middle + 1, S):
            step(j, (part,))
        own_copy(0, part).wait()
        own_copy(1, part).wait()
        q_wait(part)
        attend(part, qbufs[part], atts[part])
    if handing:
        @pl.when(outer)
        def _():
            pltpu.make_async_copy(atts[0], atts[0], a_recv.at[0]).wait()

    for i, load in enumerate(small_loads):
        if not 3 <= i < 10:
            load.wait()
    loads[0].wait()
    def p_copy(d, i):
        p = partner(d)
        span = slice(i * W, (i + 1) * W)
        return remote(
            pbuf.at[rows(p), span], prec.at[d - 1, :, span],
            p_send.at[d - 1, i], p_recv.at[d - 1, i], {"head": p},
        )

    for i in range(QUARTERS):
        span = slice(i * W, (i + 1) * W)
        pbuf[:, span] = sum(
            jnp.dot(
                atts[part][...],
                wo[parts[part][0] * HEAD_DIM : (parts[part][0] + parts[part][1]) * HEAD_DIM, span],
                preferred_element_type=F32,
            )
            for part in range(P2)
        ).astype(BF16)
        for d in range(1, H):
            p_copy(d, i).start()

    for i in range(QUARTERS):
        for d in range(1, H):
            p_copy(d, i).wait_recv()
    step_rows = 16

    def normalise(i, carry):
        r = pl.ds(pl.multiple_of(i * step_rows, step_rows), step_rows)
        total = pbuf[pl.ds(pl.multiple_of(x * T + i * step_rows, step_rows), step_rows), :].astype(F32)
        for d in range(1, H):
            total = total + prec[d - 1, r, :].astype(F32)
        h = res_ref[0, r, :].astype(F32) + mod_ref[0, 0:1, :] * total
        hidden[r, :] = h
        centered = h - jnp.mean(h, axis=-1, keepdims=True)
        variance = jnp.mean(centered * centered, axis=-1, keepdims=True)
        mixed = (
            centered * lax.rsqrt(variance + EPSILON) * (1.0 + mod_ref[0, 2:3, :]) + mod_ref[0, 1:2, :]
        ).astype(BF16)
        for q in range(QUARTERS):
            mixq[pl.ds(pl.multiple_of(q * T + i * step_rows, step_rows), step_rows), :] = mixed[
                :, q * W : (q + 1) * W
            ]
        return carry

    lax.fori_loop(0, T // step_rows, normalise, 0)

    xout[...] = jnp.dot(placing[...], mixq[...], preferred_element_type=F32).astype(BF16).reshape(E, R, W)

    def d_copy(d):
        o, device = other(d)
        return remote(xout.at[o], xin.at[x * N + me], d_send.at[d], d_recv.at[x * N + me], device)

    def dx_copy(d, o, own):
        p = partner(d)
        src = xout.at[me] if own else xin.at[x * N + o]
        return remote(src, xin.at[x * N + o], dx_send.at[d - 1, o], d_recv.at[x * N + o], {"head": p})

    def block_wait(buf, i, sem):
        pltpu.make_async_copy(buf.at[i], buf.at[i], sem).wait()

    for d in range(1, H):
        dx_copy(d, me, True).start()
    for d in range(1, N):
        d_copy(d).start()
    own_x = pltpu.make_async_copy(xout.at[me], xin.at[x * N + me], lsem.at[2, 0])
    own_x.start()
    logits = sum(
        lax.dot_general(
            mixq[q * T : (q + 1) * T, :], router_ref[:, q * W : (q + 1) * W],
            (((1,), (1,)), ((), ())), preferred_element_type=F32,
        )
        for q in range(QUARTERS)
    )
    chosen = [jnp.sum(logits * hot_col[k][:T, :], axis=1, keepdims=True) for k in range(2)]
    gates = [jax.nn.sigmoid(chosen[0] - chosen[1]), jax.nn.sigmoid(chosen[1] - chosen[0])]
    def y_copy(d, o):
        p = partner(d)
        return remote(yout.at[p * N + o], yrec.at[d - 1, o], y_send.at[d - 1, o], y_recv.at[d - 1, o], {"head": p})

    def r_copy(d):
        o = origin(d)
        device = {"seq": o // C, "cfg": lax.rem(o, C)}
        return remote(ysum.at[o], ret.at[me], r_send.at[d], r_recv.at[me], device)

    def forward(d):
        if d == 0:
            own_x.wait()
            return
        o = origin(d)
        block_wait(xin, x * N + o, d_recv.at[x * N + o])
        for e in range(1, H):
            dx_copy(e, o, False).start()

    def y_start(d):
        for e in range(1, H):
            y_copy(e, origin(d)).start()

    size = N // groups

    def finish(d):
        o = origin(d)
        total = yout[x * N + o].astype(F32)
        for e in range(1, H):
            y_copy(e, o).wait_recv()
            total = total + yrec[e - 1, o].astype(F32)
        if d:
            ysum[o] = total.astype(BF16)
            r_copy(d).start()
        else:
            ret[me] = total.astype(BF16)

    G = H * size
    g = perm_ref.shape[0] // (QUARTERS * B) if B else 1

    def mine(n):
        return list(range(n * size, (n + 1) * size))

    def expert(n):
        for e in range(1, H):
            for d in mine(n):
                slot = partner(e) * N + origin(d)
                block_wait(xin, slot, d_recv.at[slot])
        places = [partner(e) * N + origin(d) for e in range(H) for d in mine(n)]
        for i, slot in enumerate(places):
            for q in range(QUARTERS):
                if A:
                    xs[q, i * A : (i + 1) * A, :] = xin[slot, q * A : (q + 1) * A, :]
        if B:
            for i in range(G // g):
                mixed_b = jnp.concatenate(
                    [xin[slot, QUARTERS * A :, :] for slot in places[i * g : (i + 1) * g]], axis=0
                )
                mixed_b = jnp.dot(perm_ref[...], mixed_b, preferred_element_type=F32).astype(BF16)
                at = G * A + i * g * B
                for q in range(QUARTERS):
                    xs[q, at : at + g * B, :] = mixed_b[q * g * B : (q + 1) * g * B, :]
        gate_out = sum(
            jnp.dot(xs[q], wg[q * W : (q + 1) * W, :], preferred_element_type=F32) for q in range(QUARTERS)
        )
        up_out = sum(
            jnp.dot(xs[q], wu[q * W : (q + 1) * W, :], preferred_element_type=F32) for q in range(QUARTERS)
        )
        activated = (gate_out / (1.0 + jnp.exp(-gate_out)) * up_out).astype(BF16)
        for q in range(QUARTERS):
            y = jnp.dot(activated, wd[:, q * W : (q + 1) * W], preferred_element_type=F32).astype(BF16)
            for i, slot in enumerate(places):
                if A:
                    yout[slot, q * A : (q + 1) * A, :] = y[i * A : (i + 1) * A, :]
            if B:
                xs[q, G * A :, :] = y[G * A :, :]
        if B:
            for i in range(G // g):
                at = G * A + i * g * B
                mixed_b = jnp.concatenate([xs[q, at : at + g * B, :] for q in range(QUARTERS)], axis=0)
                mixed_b = jnp.dot(perm_t_ref[...], mixed_b, preferred_element_type=F32).astype(BF16)
                for k, slot in enumerate(places[i * g : (i + 1) * g]):
                    yout[slot, QUARTERS * A :, :] = mixed_b[k * QUARTERS * B : (k + 1) * QUARTERS * B, :]

    for load in loads[1:]:
        load.wait()
    actions = {"F": forward, "Y": y_start, "Z": finish}
    for step, n, i in order(groups, size):
        if step == "D":
            expert(n)
        else:
            actions[step](n * size + i)
    for d in range(1, N):
        o = other(d)[0]
        block_wait(ret, o, r_recv.at[o])

    back = ret[...].reshape(E * R, W)
    picked = [
        jnp.dot(picks[k], back, preferred_element_type=F32)
        for k in range(2)
    ]
    for q in range(QUARTERS):
        span = slice(q * W, (q + 1) * W)
        r = slice(q * T, (q + 1) * T)
        mix = gates[0] * picked[0][r, :] + gates[1] * picked[1][r, :]
        out_ref[0, :, span] = (hidden[:, span] + mod_ref[0, 3:4, span] * mix).astype(BF16)

    for part in range(P2):
        low, high = (1, S - 2) if parts[part][2] else (0, S - 1)
        for kv in range(2):
            for d in range(1, H):
                x_copy(kv, part, d).wait_send()
            for d in range(H):
                both_ways(kv, part, partner(d), d == 0, lambda copy: copy.wait_send())
            for j in range(1, S):
                for d in range(H):
                    ox = partner(d)

                    @pl.when((z - j >= 0) & (z + 1 <= high))
                    def _():
                        z_copy(kv, part, ox, z - j, 1, False).wait_send()

                    @pl.when((z + j < S) & (z - 1 >= low))
                    def _():
                        z_copy(kv, part, ox, z + j, -1, False).wait_send()
        if not parts[part][2]:
            for d in range(1, H):
                q_copy(part, d).wait_send()
    if handing:
        @pl.when(inner)
        def _():
            for d in range(1, H):
                q_copy(0, d).wait_send()

        @pl.when(outer)
        def _():
            for d in range(H):
                hand_copy(d).wait_send()

        @pl.when(helping)
        def _():
            give_back().wait_send()
    for d in range(1, H):
        for i in range(QUARTERS):
            p_copy(d, i).wait_send()
        dx_copy(d, me, True).wait_send()
        for o in range(N):
            y_copy(d, o).wait_send()
        for i in range(1, N):
            dx_copy(d, other(i)[0], False).wait_send()
    for d in range(1, N):
        d_copy(d).wait_send()
        r_copy(d).wait_send()


def solution(mesh):
    S, H, C = mesh.shape["seq"], mesh.shape["head"], mesh.shape["cfg"]
    N = S * C

    def local(
        residual, queries, key_rows, value_rows, out_weight, modulation, router,
        gate_weight, up_weight, down_weight, expert_ids,
    ):
        T, D = residual.shape[1:]
        F = queries.shape[2] // H
        E, FF = router.shape[1], gate_weight.shape[2]
        top = expert_ids.shape[2]
        capacity = max(2, (5 * top * T + 4 * E - 1) // (4 * E))
        A = capacity // 16 * 16
        B = -(-(capacity - A) // 4) * 4
        R, W, G = QUARTERS * (A + B), D // QUARTERS, H * N
        slots = A + B
        groups = 4 if S % 4 == 0 else 2 if S % 2 == 0 else 1
        group = G // groups
        key = np.zeros((E, R), np.float32)
        for e in range(E):
            for q in range(QUARTERS):
                first = q * E * slots + e * slots
                key[e, q * A : (q + 1) * A] = first + np.arange(A)
                at = QUARTERS * A + q * B
                key[e, at : at + B] = first + A + np.arange(B)
        key = key.reshape(E * R)
        upper = np.tile(np.triu(np.ones((T, T), np.float32), 1), (1, QUARTERS))
        perm = np.eye(8, dtype=np.float32)
        if B:
            g = max(n for n in range(1, group + 1) if group % n == 0 and n * QUARTERS * B <= 256)
            size = g * QUARTERS * B
            place = np.arange(size).reshape(g, QUARTERS, B).transpose(1, 0, 2).reshape(-1)
            perm = np.zeros((size, size), np.float32)
            perm[np.arange(size), place] = 1.0
        tiled = np.tile(np.eye(T, dtype=np.float32), (1, QUARTERS))
        heads = F // HEAD_DIM
        early = max(1, heads // 3) if heads > 1 else 0
        parts = ((0, early, S >= 4), (early, heads - early, False)) if early else ((0, heads, False),)
        widths = [count * HEAD_DIM for _, count, _ in parts]
        P2 = len(parts)
        sizes = (S, H, C, T, F, D, E, A, B, R, parts, groups)
        keys = H * S * T
        hbm, vmem = pl.BlockSpec(memory_space=pl.ANY), pl.BlockSpec(memory_space=pltpu.VMEM)
        dma = pltpu.SemaphoreType.DMA
        V = pltpu.VMEM
        small = (
            residual, modulation, router.T, expert_ids[0].T,
            jnp.asarray(tiled, BF16), jnp.asarray(tiled.T, BF16),
            jnp.asarray(upper, BF16), jnp.asarray(upper.T, BF16),
            jnp.asarray(key[:, None]), jnp.asarray(key[None, :]),
            jnp.asarray(perm, BF16), jnp.asarray(perm.T, BF16),
        )
        out = pl.pallas_call(
            functools.partial(kernel, sizes),
            out_shape=jax.ShapeDtypeStruct((1, T, D), BF16),
            in_specs=[hbm] * (7 + len(small)),
            out_specs=vmem,
            scratch_shapes=[
                *(V(a.shape, a.dtype) for a in small),
                *(V((keys, w), BF16) for w in widths), *(V((keys, w), BF16) for w in widths),
                *(V((H * T, w), BF16) for w in widths), *(V((H * T, w), BF16) for w in widths),
                V((H * T, widths[0]), BF16),
                V((F, D), BF16), V((D, FF), BF16), V((D, FF), BF16), V((FF, D), BF16),
                V((H * T, D), BF16), V((H - 1, T, D), BF16),
                V((T, D), F32), V((QUARTERS * T, W), BF16),
                V((E, R, W), BF16), V((G, R, W), BF16), V((QUARTERS, group * slots, W), BF16),
                V((G, R, W), BF16), V((H - 1, N, R, W), BF16),
                V((N, R, W), BF16), V((E, R, W), BF16),
                V((E * R, QUARTERS * T), BF16), V((2, QUARTERS * T, E * R), BF16),
                dma((len(small),)), dma((3, P2)), dma((4,)),
                dma((2, P2, H * S)), dma((2, P2, H - 1)), dma((2, P2, H * S, 2)),
                dma((P2, H - 1)), dma((P2, H)), dma((H,)), dma((H,)), dma((1,)), dma((1,)),
                dma((H - 1, QUARTERS)), dma((H - 1, QUARTERS)),
                dma((N,)), dma((G,)), dma((H - 1, N)), dma((H - 1, N)), dma((H - 1, N)),
                dma((N,)), dma((N,)),
            ],
            compiler_params=pltpu.CompilerParams(
                collective_id=0, has_side_effects=True, vmem_limit_bytes=63000 * 1024
            ),
        )(
            queries[0], key_rows[0], value_rows[0], out_weight, gate_weight, up_weight, down_weight, *small
        )
        return out

    rows = P("cfg", ("group", "seq", "head"), None)
    return jax.shard_map(
        local,
        mesh=mesh,
        in_specs=(
            rows, rows, rows, rows,
            P("head", None),
            P("cfg", "group", None),
            P(),
            P(("seq", "cfg"), None, "head"),
            P(("seq", "cfg"), None, "head"),
            P(("seq", "cfg"), "head", None),
            rows,
        ),
        out_specs=rows,
        check_vma=False,
    )
```

```python
import functools
import jax
import jax.numpy as jnp
import numpy as np
from jax import lax
from jax.experimental import pallas as pl
from jax.experimental.pallas import tpu as pltpu
from jax.sharding import PartitionSpec as P

HEAD_DIM = 128
EPSILON = 1e-06
QUARTERS = 4
MESH = pl.DeviceIdType.MESH
F32 = jnp.float32
BF16 = jnp.bfloat16


def order(groups, size):
    def every(step, n):
        return [(step, n, d) for d in range(size)]

    if groups == 1:
        return every("F", 0) + [("D", 0, -1)] + every("Y", 0) + every("Z", 0)
    if groups == 2:
        return (
            every("F", 0) + [("D", 0, -1)] + every("F", 1) + every("Y", 0) + [("D", 1, -1)]
            + every("Y", 1) + every("Z", 1) + every("Z", 0)
        )
    if size != 2:
        steps = every("F", 0) + every("F", 1) + every("F", 2) + every("F", 3)
        for n in (1, 2, 3, 0):
            steps += [("D", n, -1)] + every("Y", n)
        return steps + every("Z", 1) + every("Z", 2) + every("Z", 3) + every("Z", 0)
    return [
        ("F", 0, 1), ("F", 1, 1), ("F", 2, 0), ("F", 1, 0), ("F", 2, 1), ("F", 0, 0), ("D", 1, 1),
        ("Y", 1, 1), ("F", 3, 1), ("D", 1, 0), ("Z", 1, 1), ("Y", 1, 0), ("F", 3, 0), ("D", 3, 1),
        ("Z", 1, 0), ("Y", 3, 1), ("D", 2, -1), ("Y", 2, 0), ("D", 3, 0), ("Z", 3, 1), ("Y", 3, 0),
        ("D", 0, -1), ("Y", 2, 1), ("Z", 2, 0), ("Z", 3, 0), ("Y", 0, 0), ("Y", 0, 1), ("Z", 2, 1),
        ("Z", 0, 0), ("Z", 0, 1),
    ]


def send_order(S, C):
    if (S, C) != (4, 2):
        return [0, *range(C, min(2 * C, S * C)), *range(1, C), *range(2 * C, S * C)]
    return [0, 3, 4, 1, 2, 5, 7, 6]


def kernel(
    sizes,
    q_hbm, k_hbm, v_hbm, wo_hbm, wg_hbm, wu_hbm, wd_hbm, *rest
):
    S, H, C, T, F, D, E, A, B, R, parts, groups = sizes
    small = 12
    small_hbm, out_ref, rest = rest[:small], rest[small], rest[small + 1 :]
    small_ref, rest = rest[:small], rest[small:]
    (res_ref, mod_ref, router_ref, ids_ref, tile_ref, tile_t_ref,
     upper_ref, lower_ref, rowkey_ref, rowkey_t_ref, perm_ref, perm_t_ref) = small_ref
    P2 = len(parts)
    kbufs, rest = rest[:P2], rest[P2:]
    vbufs, rest = rest[:P2], rest[P2:]
    qbufs, rest = rest[:P2], rest[P2:]
    atts, rest = rest[:P2], rest[P2:]
    (hand, wo, wg, wu, wd,
     pbuf, prec, hidden, mixq,
     xout, xin, xs, yout, yrec, ysum, ret, placing, picks,
     ssem, lsem, wsem, kv_recv, kv_xsend, kv_zsend, q_send, q_recv, h_send, h_recv, a_send, a_recv,
     p_send, p_recv, d_send, d_recv, dx_send, y_send, y_recv, r_send, r_recv, result, osem) = rest
    N = S * C
    W = D // QUARTERS
    z, x, c = lax.axis_index("seq"), lax.axis_index("head"), lax.axis_index("cfg")
    me = z * C + c
    handing = any(p[2] for p in parts)

    small_loads = [pltpu.make_async_copy(a, b, ssem.at[i]) for i, (a, b) in enumerate(zip(small_hbm, small_ref))]
    for load in small_loads:
        load.start()

    def partner(d):
        return lax.rem(x + d, H)

    half = S // 2

    def near(n):
        if S % 2:
            return lax.rem(z + n, S)
        side = lax.rem(z // half + n % 2, 2)
        return side * half + lax.rem(lax.rem(z, half) + n // 2, half)

    def other(d):
        to_z, to_c = near(d // C), lax.rem(c + d % C, C)
        return to_z * C + to_c, {"seq": to_z, "cfg": to_c}

    def origin(d):
        return near(d // C) * C + lax.rem(c - d % C + C, C)

    def rows(i):
        return pl.ds(pl.multiple_of(i * T, T), T)

    def remote(src, dst, send, recv, device):
        return pltpu.make_async_remote_copy(
            src_ref=src, dst_ref=dst, send_sem=send, recv_sem=recv,
            device_id=device, device_id_type=MESH,
        )

    barrier = pltpu.get_barrier_semaphore()

    def greet(device):
        pl.semaphore_signal(barrier, inc=1, device_id=device, device_id_type=MESH)

    for d in range(1, H):
        greet({"head": partner(d)})
    for d in range(1, C):
        greet({"cfg": lax.rem(c + d, C)})
    for d in range(H):
        @pl.when(z < S - 1)
        def _():
            greet({"seq": z + 1, "head": partner(d)})

        @pl.when(z > 0)
        def _():
            greet({"seq": z - 1, "head": partner(d)})

    sides = jnp.where(z < S - 1, 1, 0) + jnp.where(z > 0, 1, 0)
    pl.semaphore_wait(barrier, H - 1 + C - 1 + H * sides)

    kv_src, kv_buf = (k_hbm, v_hbm), (kbufs, vbufs)
    outer = (z == 0) | (z == S - 1)
    inner = jnp.logical_not(outer)
    helping = (z == 1) | (z == S - 2)
    helper = jnp.where(z == 0, 1, S - 2)
    helped = jnp.where(z == 1, 0, S - 1)

    def cols(part, p):
        first, count, _ = parts[part]
        return pl.ds(pl.multiple_of(p * F + first * HEAD_DIM, 128), count * HEAD_DIM)

    def x_copy(kv, part, d):
        p = partner(d)
        return remote(
            kv_src[kv].at[:, cols(part, p)], kv_buf[kv][part].at[rows(x * S + z)],
            kv_xsend.at[kv, part, d - 1], kv_recv.at[kv, part, x * S + z], {"head": p},
        )

    def own_copy(kv, part):
        return pltpu.make_async_copy(
            kv_src[kv].at[:, cols(part, x)], kv_buf[kv][part].at[rows(x * S + z)], lsem.at[kv, part]
        )

    def z_copy(kv, part, ox, oz, step, own):
        block = ox * S + oz
        src = kv_src[kv].at[:, cols(part, x)] if own else kv_buf[kv][part].at[rows(block)]
        return remote(
            src, kv_buf[kv][part].at[rows(block)],
            kv_zsend.at[kv, part, block, 0 if step > 0 else 1], kv_recv.at[kv, part, block],
            {"seq": z + step},
        )

    def right(part):
        return z + 1 <= (S - 2 if parts[part][2] else S - 1)

    def leftward(part):
        return z - 1 >= (1 if parts[part][2] else 0)

    def both_ways(kv, part, ox, own, act):
        @pl.when(right(part))
        def _():
            act(z_copy(kv, part, ox, z, 1, own))

        @pl.when(leftward(part))
        def _():
            act(z_copy(kv, part, ox, z, -1, own))

    def q_copy(part, d):
        p = partner(d)
        return remote(
            q_hbm.at[:, cols(part, p)], qbufs[part].at[rows(x)],
            q_send.at[part, d - 1], q_recv.at[part, x], {"head": p},
        )

    def own_q(part):
        return pltpu.make_async_copy(q_hbm.at[:, cols(part, x)], qbufs[part].at[rows(x)], lsem.at[2, part])

    def hand_copy(d):
        p = partner(d)
        return remote(
            q_hbm.at[:, cols(0, p)], hand.at[rows(x)],
            h_send.at[d], h_recv.at[x], {"seq": helper, "head": p},
        )

    def give_back():
        return remote(hand, atts[0], a_send.at[0], a_recv.at[0], {"seq": helped})

    def q_start(part):
        if parts[part][2]:
            @pl.when(inner)
            def _():
                for d in range(1, H):
                    q_copy(part, d).start()
                own_q(part).start()

            @pl.when(outer)
            def _():
                for d in range(H):
                    hand_copy(d).start()
        else:
            for d in range(1, H):
                q_copy(part, d).start()
            own_q(part).start()

    def q_wait(part):
        own_q(part).wait()
        for d in range(1, H):
            p = partner(d)
            pltpu.make_async_copy(
                qbufs[part].at[rows(p)], qbufs[part].at[rows(p)], q_recv.at[part, p]
            ).wait()

    def begin(part):
        for kv in range(2):
            for d in range(1, H):
                x_copy(kv, part, d).start()
            both_ways(kv, part, x, True, lambda copy: copy.start())

    for part in range(P2):
        begin(part)
    for part in range(P2):
        q_start(part)
    for part in range(P2):
        for kv in range(2):
            own_copy(kv, part).start()
    loads = [
        pltpu.make_async_copy(a, b, wsem.at[i])
        for i, (a, b) in enumerate(((wo_hbm, wo), (wg_hbm.at[0], wg), (wu_hbm.at[0], wu), (wd_hbm.at[0], wd)))
    ]
    for load in loads:
        load.start()

    def arrived(kv, part, block):
        pltpu.make_async_copy(
            kv_buf[kv][part].at[rows(block)], kv_buf[kv][part].at[rows(block)], kv_recv.at[kv, part, block]
        ).wait()

    def relay(kv, part, j):
        if j == 0:
            for d in range(1, H):
                ox = partner(d)
                arrived(kv, part, ox * S + z)
                both_ways(kv, part, ox, False, lambda copy: copy.start())
            return
        low, high = (1, S - 2) if parts[part][2] else (0, S - 1)
        for d in range(H):
            ox = partner(d)

            @pl.when((z - j >= 0) & (z <= high))
            def _():
                arrived(kv, part, ox * S + z - j)

                @pl.when(z + 1 <= high)
                def _():
                    z_copy(kv, part, ox, z - j, 1, False).start()

            @pl.when((z + j < S) & (z >= low))
            def _():
                arrived(kv, part, ox * S + z + j)

                @pl.when(z - 1 >= low)
                def _():
                    z_copy(kv, part, ox, z + j, -1, False).start()

    for load in small_loads[3:10]:
        load.wait()
    ids = ids_ref[...].astype(F32).astype(BF16)
    ids_row = jnp.dot(ids, tile_ref[...], preferred_element_type=F32)
    ids_col = lax.dot_general(tile_t_ref[...], ids, (((1,), (1,)), ((), ())), preferred_element_type=F32)
    expert_rows = lax.broadcasted_iota(jnp.int32, (E, QUARTERS * T), 0).astype(F32)
    hot_row = [(ids_row[k : k + 1, :] == expert_rows).astype(F32) for k in range(2)]
    named = (hot_row[0] + hot_row[1])[:, :T].astype(BF16)
    earlier = jnp.dot(named, upper_ref[...], preferred_element_type=F32)
    slots = A + B
    quarter_row = (lax.broadcasted_iota(jnp.int32, (1, QUARTERS * T), 1) // T * (E * slots)).astype(F32)
    key_row = [
        quarter_row
        + ids_row[k : k + 1, :] * slots
        + jnp.sum(earlier * hot_row[k], axis=0, keepdims=True)
        for k in range(2)
    ]
    expert_cols = lax.broadcasted_iota(jnp.int32, (QUARTERS * T, E), 1).astype(F32)
    hot_col = [(ids_col[:, k : k + 1] == expert_cols).astype(F32) for k in range(2)]
    named = (hot_col[0] + hot_col[1])[:T, :].astype(BF16)
    earlier = jnp.dot(lower_ref[...], named, preferred_element_type=F32)
    quarter_col = (lax.broadcasted_iota(jnp.int32, (QUARTERS * T, 1), 0) // T * (E * slots)).astype(F32)
    key_col = [
        quarter_col
        + ids_col[:, k : k + 1] * slots
        + jnp.sum(earlier * hot_col[k], axis=1, keepdims=True)
        for k in range(2)
    ]

    placing[...] = (
        (rowkey_ref[...] == key_row[0]).astype(F32) + (rowkey_ref[...] == key_row[1]).astype(F32)
    ).astype(BF16)
    for k in range(2):
        picks[k] = (key_col[k] == rowkey_t_ref[...]).astype(BF16)

    heads = F // HEAD_DIM
    block_rows = H * T if H * T * H * S * T <= 131072 else T
    blocks = H * T // block_rows
    factor = HEAD_DIM ** (-0.5)

    def over_blocks(body):
        if blocks == 1:
            body(slice(0, block_rows))
        else:
            def step(i, carry):
                body(pl.ds(pl.multiple_of(i * block_rows, block_rows), block_rows))
                return carry

            lax.fori_loop(0, blocks, step, 0)


    def score(part, q, r, h):
        span = slice(h * HEAD_DIM, (h + 1) * HEAD_DIM)
        s = lax.dot_general(
            q[r, span], kbufs[part][:, span], (((1,), (1,)), ((), ())), preferred_element_type=F32,
        ) * factor
        w = jnp.exp(s - jnp.max(s, axis=1, keepdims=True))
        return w.astype(BF16), jnp.sum(w, axis=1, keepdims=True)

    def attend(part, q, out, r):
        for h in range(parts[part][1]):
            span = slice(h * HEAD_DIM, (h + 1) * HEAD_DIM)
            w, total = score(part, q, r, h)
            u = jnp.dot(w, vbufs[part][:, span], preferred_element_type=F32)
            out[r, span] = (u / total).astype(BF16)

    def attend_all(part, q, out):
        over_blocks(lambda r: attend(part, q, out, r))

    def early():
        own_copy(0, 0).wait()
        own_copy(1, 0).wait()
        if parts[0][2]:
            @pl.when(helping)
            def _():
                for d in range(H):
                    p = partner(d)
                    pltpu.make_async_copy(hand.at[rows(p)], hand.at[rows(p)], h_recv.at[p]).wait()
                attend_all(0, hand, hand)
                give_back().start()

            @pl.when(inner)
            def _():
                q_wait(0)
                attend_all(0, qbufs[0], atts[0])
        else:
            q_wait(0)
            attend_all(0, qbufs[0], atts[0])

    def step(j, among):
        for part in among:
            for kv in range(2):
                relay(kv, part, j)

    middle = S // 2 if P2 > 1 else S - 1
    for j in range(middle + 1):
        step(j, range(P2))
    for j in range(middle + 1, S):
        step(j, range(1))
    early()
    for part in range(1, P2):
        for j in range(middle + 1, S):
            step(j, (part,))
        own_copy(0, part).wait()
        own_copy(1, part).wait()
        q_wait(part)
    if handing:
        @pl.when(outer)
        def _():
            pltpu.make_async_copy(atts[0], atts[0], a_recv.at[0]).wait()

    for i, load in enumerate(small_loads):
        if not 3 <= i < 10:
            load.wait()
    loads[0].wait()

    step_rows = 16
    slices = T // step_rows

    def p_copy(d, i):
        p, s = partner(d), max(0, i - QUARTERS + 1)
        span = slice(i * W, (i + 1) * W) if i < QUARTERS else slice(0, D)
        return remote(
            pbuf.at[pl.ds(pl.multiple_of(p * T + s * step_rows, step_rows), step_rows), span],
            prec.at[d - 1, pl.ds(s * step_rows, step_rows), span],
            p_send.at[d - 1, i], p_recv.at[d - 1, i], {"head": p},
        )

    def project(p, span):
        pbuf[rows(p), span] = sum(
            jnp.dot(
                atts[part][rows(p), :],
                wo[parts[part][0] * HEAD_DIM : (parts[part][0] + parts[part][1]) * HEAD_DIM, span],
                preferred_element_type=F32,
            )
            for part in range(P2)
        ).astype(BF16)

    for d in [*range(1, H), 0]:
        p = partner(d)
        for part in range(1, P2):
            attend(part, qbufs[part], atts[part], rows(p))
        for i in range(QUARTERS):
            project(p, slice(i * W, (i + 1) * W))
            if d:
                p_copy(d, i).start()
        if d:
            for i in range(QUARTERS, QUARTERS + slices - 1):
                p_copy(d, i).start()

    def normalise(i):
        r = pl.ds(pl.multiple_of(i * step_rows, step_rows), step_rows)
        total = pbuf[pl.ds(pl.multiple_of(x * T + i * step_rows, step_rows), step_rows), :].astype(F32)
        for d in range(1, H):
            total = total + prec[d - 1, r, :].astype(F32)
        h = res_ref[0, r, :].astype(F32) + mod_ref[0, 0:1, :] * total
        hidden[r, :] = h
        centered = h - jnp.mean(h, axis=-1, keepdims=True)
        variance = jnp.mean(centered * centered, axis=-1, keepdims=True)
        mixed = (
            centered * lax.rsqrt(variance + EPSILON) * (1.0 + mod_ref[0, 2:3, :]) + mod_ref[0, 1:2, :]
        ).astype(BF16)
        for q in range(QUARTERS):
            mixq[pl.ds(pl.multiple_of(q * T + i * step_rows, step_rows), step_rows), :] = mixed[
                :, q * W : (q + 1) * W
            ]

    for s in range(slices):
        for d in range(1, H):
            for i in range(QUARTERS) if s == 0 else (QUARTERS + s - 1,):
                p_copy(d, i).wait_recv()
        normalise(s)

    def d_copy(d):
        o, device = other(d)
        return remote(xout.at[o], xin.at[x * N + me], d_send.at[d], d_recv.at[x * N + me], device)

    def dx_copy(d, o, own):
        p = partner(d)
        src = xout.at[me] if own else xin.at[x * N + o]
        return remote(src, xin.at[x * N + o], dx_send.at[d - 1, o], d_recv.at[x * N + o], {"head": p})

    def block_wait(buf, i, sem):
        pltpu.make_async_copy(buf.at[i], buf.at[i], sem).wait()

    own_x = pltpu.make_async_copy(xout.at[me], xin.at[x * N + me], lsem.at[2, 0])
    for d in send_order(S, C):
        o = other(d)[0]
        xout[o] = jnp.dot(
            placing[pl.ds(pl.multiple_of(o * R, 16), R), :], mixq[...], preferred_element_type=F32
        ).astype(BF16)
        if d:
            d_copy(d).start()
        else:
            for e in range(1, H):
                dx_copy(e, me, True).start()
            own_x.start()
    logits = sum(
        lax.dot_general(
            mixq[q * T : (q + 1) * T, :], router_ref[:, q * W : (q + 1) * W],
            (((1,), (1,)), ((), ())), preferred_element_type=F32,
        )
        for q in range(QUARTERS)
    )
    chosen = [jnp.sum(logits * hot_col[k][:T, :], axis=1, keepdims=True) for k in range(2)]
    gates = [jax.nn.sigmoid(chosen[0] - chosen[1]), jax.nn.sigmoid(chosen[1] - chosen[0])]
    def y_copy(d, o):
        p = partner(d)
        return remote(yout.at[p * N + o], yrec.at[d - 1, o], y_send.at[d - 1, o], y_recv.at[d - 1, o], {"head": p})

    def r_copy(d):
        o = origin(d)
        device = {"seq": o // C, "cfg": lax.rem(o, C)}
        return remote(ysum.at[o], ret.at[me], r_send.at[d], r_recv.at[me], device)

    def forward(d):
        if d == 0:
            own_x.wait()
            return
        o = origin(d)
        block_wait(xin, x * N + o, d_recv.at[x * N + o])
        for e in range(1, H):
            dx_copy(e, o, False).start()

    def y_start(d):
        for e in range(1, H):
            y_copy(e, origin(d)).start()

    size = N // groups

    def finish(d):
        o = origin(d)
        total = yout[x * N + o].astype(F32)
        for e in range(1, H):
            y_copy(e, o).wait_recv()
            total = total + yrec[e - 1, o].astype(F32)
        if d:
            ysum[o] = total.astype(BF16)
            r_copy(d).start()
        else:
            ret[me] = total.astype(BF16)

    g = perm_ref.shape[0] // (QUARTERS * B) if B else 1

    def mine(n):
        return list(range(n * size, (n + 1) * size))

    def expert(chosen):
        for e in range(1, H):
            for d in chosen:
                slot = partner(e) * N + origin(d)
                block_wait(xin, slot, d_recv.at[slot])
        places = [partner(e) * N + origin(d) for e in range(H) for d in chosen]
        for i, slot in enumerate(places):
            for q in range(QUARTERS):
                if A:
                    xs[q, i * A : (i + 1) * A, :] = xin[slot, q * A : (q + 1) * A, :]
        base = len(places) * A
        bundles = [(places[i : i + g] * g)[:g] for i in range(0, len(places), g)] if B else []
        for i, bundle in enumerate(bundles):
            mixed_b = jnp.concatenate([xin[slot, QUARTERS * A :, :] for slot in bundle], axis=0)
            mixed_b = jnp.dot(perm_ref[...], mixed_b, preferred_element_type=F32).astype(BF16)
            at = base + i * g * B
            for q in range(QUARTERS):
                xs[q, at : at + g * B, :] = mixed_b[q * g * B : (q + 1) * g * B, :]
        total = base + len(bundles) * g * B
        gate_out = sum(
            jnp.dot(xs[q, :total, :], wg[q * W : (q + 1) * W, :], preferred_element_type=F32)
            for q in range(QUARTERS)
        )
        up_out = sum(
            jnp.dot(xs[q, :total, :], wu[q * W : (q + 1) * W, :], preferred_element_type=F32)
            for q in range(QUARTERS)
        )
        activated = (gate_out / (1.0 + jnp.exp(-gate_out)) * up_out).astype(BF16)
        for q in range(QUARTERS):
            y = jnp.dot(activated, wd[:, q * W : (q + 1) * W], preferred_element_type=F32).astype(BF16)
            for i, slot in enumerate(places):
                if A:
                    yout[slot, q * A : (q + 1) * A, :] = y[i * A : (i + 1) * A, :]
            if B:
                xs[q, base:total, :] = y[base:, :]
        for i, bundle in enumerate(bundles):
            at = base + i * g * B
            mixed_b = jnp.concatenate([xs[q, at : at + g * B, :] for q in range(QUARTERS)], axis=0)
            mixed_b = jnp.dot(perm_t_ref[...], mixed_b, preferred_element_type=F32).astype(BF16)
            for k, slot in enumerate(places[i * g : (i + 1) * g]):
                yout[slot, QUARTERS * A :, :] = mixed_b[k * QUARTERS * B : (k + 1) * QUARTERS * B, :]

    for load in loads[1:]:
        load.wait()
    actions = {"F": forward, "Y": y_start, "Z": finish}
    for step, n, i in order(groups, size):
        if step == "D":
            expert(mine(n) if i < 0 else [n * size + i])
        else:
            actions[step](n * size + i)
    for d in range(1, N):
        o = other(d)[0]
        block_wait(ret, o, r_recv.at[o])

    def out_copy(q):
        span = slice(q * W, (q + 1) * W)
        return pltpu.make_async_copy(result.at[:, span], out_ref.at[0, :, span], osem.at[q])

    back = ret[...].reshape(E * R, W)
    picked = [
        jnp.dot(picks[k], back, preferred_element_type=F32)
        for k in range(2)
    ]
    for q in range(QUARTERS):
        span = slice(q * W, (q + 1) * W)
        r = slice(q * T, (q + 1) * T)
        mix = gates[0] * picked[0][r, :] + gates[1] * picked[1][r, :]
        result[:, span] = (hidden[:, span] + mod_ref[0, 3:4, span] * mix).astype(BF16)
        out_copy(q).start()
    for q in range(QUARTERS):
        out_copy(q).wait()

    for part in range(P2):
        low, high = (1, S - 2) if parts[part][2] else (0, S - 1)
        for kv in range(2):
            for d in range(1, H):
                x_copy(kv, part, d).wait_send()
            for d in range(H):
                both_ways(kv, part, partner(d), d == 0, lambda copy: copy.wait_send())
            for j in range(1, S):
                for d in range(H):
                    ox = partner(d)

                    @pl.when((z - j >= 0) & (z + 1 <= high))
                    def _():
                        z_copy(kv, part, ox, z - j, 1, False).wait_send()

                    @pl.when((z + j < S) & (z - 1 >= low))
                    def _():
                        z_copy(kv, part, ox, z + j, -1, False).wait_send()
        if not parts[part][2]:
            for d in range(1, H):
                q_copy(part, d).wait_send()
    if handing:
        @pl.when(inner)
        def _():
            for d in range(1, H):
                q_copy(0, d).wait_send()

        @pl.when(outer)
        def _():
            for d in range(H):
                hand_copy(d).wait_send()

        @pl.when(helping)
        def _():
            give_back().wait_send()
    for d in range(1, H):
        for i in range(QUARTERS + slices - 1):
            p_copy(d, i).wait_send()
        dx_copy(d, me, True).wait_send()
        for o in range(N):
            y_copy(d, o).wait_send()
        for i in range(1, N):
            dx_copy(d, other(i)[0], False).wait_send()
    for d in range(1, N):
        d_copy(d).wait_send()
        r_copy(d).wait_send()


def solution(mesh):
    S, H, C = mesh.shape["seq"], mesh.shape["head"], mesh.shape["cfg"]
    N = S * C

    def local(
        residual, queries, key_rows, value_rows, out_weight, modulation, router,
        gate_weight, up_weight, down_weight, expert_ids,
    ):
        T, D = residual.shape[1:]
        F = queries.shape[2] // H
        E, FF = router.shape[1], gate_weight.shape[2]
        top = expert_ids.shape[2]
        capacity = max(2, (5 * top * T + 4 * E - 1) // (4 * E))
        A = capacity // 16 * 16
        B = -(-(capacity - A) // 4) * 4
        R, W, G = QUARTERS * (A + B), D // QUARTERS, H * N
        slots = A + B
        groups = 4 if S % 4 == 0 else 2 if S % 2 == 0 else 1
        group = G // groups
        key = np.zeros((E, R), np.float32)
        for e in range(E):
            for q in range(QUARTERS):
                first = q * E * slots + e * slots
                key[e, q * A : (q + 1) * A] = first + np.arange(A)
                at = QUARTERS * A + q * B
                key[e, at : at + B] = first + A + np.arange(B)
        key = key.reshape(E * R)
        upper = np.tile(np.triu(np.ones((T, T), np.float32), 1), (1, QUARTERS))
        perm = np.eye(8, dtype=np.float32)
        if B:
            g = max(n for n in range(1, group + 1) if group % n == 0 and n * QUARTERS * B <= 256)
            size = g * QUARTERS * B
            place = np.arange(size).reshape(g, QUARTERS, B).transpose(1, 0, 2).reshape(-1)
            perm = np.zeros((size, size), np.float32)
            perm[np.arange(size), place] = 1.0
        tiled = np.tile(np.eye(T, dtype=np.float32), (1, QUARTERS))
        heads = F // HEAD_DIM
        early = max(1, heads // 3) if heads > 1 else 0
        parts = ((0, early, S >= 4), (early, heads - early, False)) if early else ((0, heads, False),)
        widths = [count * HEAD_DIM for _, count, _ in parts]
        P2 = len(parts)
        sizes = (S, H, C, T, F, D, E, A, B, R, parts, groups)
        keys = H * S * T
        hbm, vmem = pl.BlockSpec(memory_space=pl.ANY), pl.BlockSpec(memory_space=pltpu.VMEM)
        dma = pltpu.SemaphoreType.DMA
        V = pltpu.VMEM
        small = (
            residual, modulation, router.T, expert_ids[0].T,
            jnp.asarray(tiled, BF16), jnp.asarray(tiled.T, BF16),
            jnp.asarray(upper, BF16), jnp.asarray(upper.T, BF16),
            jnp.asarray(key[:, None]), jnp.asarray(key[None, :]),
            jnp.asarray(perm, BF16), jnp.asarray(perm.T, BF16),
        )
        out = pl.pallas_call(
            functools.partial(kernel, sizes),
            out_shape=jax.ShapeDtypeStruct((1, T, D), BF16),
            in_specs=[hbm] * (7 + len(small)),
            out_specs=hbm,
            scratch_shapes=[
                *(V(a.shape, a.dtype) for a in small),
                *(V((keys, w), BF16) for w in widths), *(V((keys, w), BF16) for w in widths),
                *(V((H * T, w), BF16) for w in widths), *(V((H * T, w), BF16) for w in widths),
                V((H * T, widths[0]), BF16),
                V((F, D), BF16), V((D, FF), BF16), V((D, FF), BF16), V((FF, D), BF16),
                V((H * T, D), BF16), V((H - 1, T, D), BF16),
                V((T, D), F32), V((QUARTERS * T, W), BF16),
                V((E, R, W), BF16), V((G, R, W), BF16), V((QUARTERS, group * slots, W), BF16),
                V((G, R, W), BF16), V((H - 1, N, R, W), BF16),
                V((N, R, W), BF16), V((E, R, W), BF16),
                V((E * R, QUARTERS * T), BF16), V((2, QUARTERS * T, E * R), BF16),
                dma((len(small),)), dma((3, P2)), dma((4,)),
                dma((2, P2, H * S)), dma((2, P2, H - 1)), dma((2, P2, H * S, 2)),
                dma((P2, H - 1)), dma((P2, H)), dma((H,)), dma((H,)), dma((1,)), dma((1,)),
                dma((H - 1, QUARTERS + T // 16 - 1)), dma((H - 1, QUARTERS + T // 16 - 1)),
                dma((N,)), dma((G,)), dma((H - 1, N)), dma((H - 1, N)), dma((H - 1, N)),
                dma((N,)), dma((N,)), V((T, D), BF16), dma((QUARTERS,)),
            ],
            compiler_params=pltpu.CompilerParams(
                collective_id=0, has_side_effects=True, vmem_limit_bytes=63000 * 1024
            ),
        )(
            queries[0], key_rows[0], value_rows[0], out_weight, gate_weight, up_weight, down_weight, *small
        )
        return out

    rows = P("cfg", ("group", "seq", "head"), None)
    return jax.shard_map(
        local,
        mesh=mesh,
        in_specs=(
            rows, rows, rows, rows,
            P("head", None),
            P("cfg", "group", None),
            P(),
            P(("seq", "cfg"), None, "head"),
            P(("seq", "cfg"), None, "head"),
            P(("seq", "cfg"), "head", None),
            rows,
        ),
        out_specs=rows,
        check_vma=False,
    )
```

```python
import functools
import jax
import jax.numpy as jnp
import numpy as np
from jax import lax
from jax.experimental import pallas as pl
from jax.experimental.pallas import tpu as pltpu
from jax.sharding import PartitionSpec as P

HEAD_DIM = 128
EPSILON = 1e-06
QUARTERS = 4
MESH = pl.DeviceIdType.MESH
F32 = jnp.float32
BF16 = jnp.bfloat16


def order(groups, size):
    def every(step, n):
        return [(step, n, d) for d in range(size)]

    if groups == 1:
        return every("F", 0) + [("D", 0, -1)] + every("Y", 0) + every("Z", 0)
    if groups == 2:
        return (
            every("F", 0) + [("D", 0, -1)] + every("F", 1) + every("Y", 0) + [("D", 1, -1)]
            + every("Y", 1) + every("Z", 1) + every("Z", 0)
        )
    if size != 2:
        steps = every("F", 0) + every("F", 1) + every("F", 2) + every("F", 3)
        for n in (1, 2, 3, 0):
            steps += [("D", n, -1)] + every("Y", n)
        return steps + every("Z", 1) + every("Z", 2) + every("Z", 3) + every("Z", 0)
    return [
        ("F", 0, 1), ("F", 1, 1), ("F", 2, 0), ("F", 1, 0), ("F", 2, 1), ("F", 0, 0), ("D", 1, 1),
        ("Y", 1, 1), ("F", 3, 1), ("D", 1, 0), ("Z", 1, 1), ("Y", 1, 0), ("F", 3, 0), ("D", 3, 1),
        ("Z", 1, 0), ("Y", 3, 1), ("D", 2, -1), ("Y", 2, 0), ("D", 3, 0), ("Z", 3, 1), ("Y", 3, 0),
        ("D", 0, -1), ("Y", 2, 1), ("Z", 2, 0), ("Z", 3, 0), ("Y", 0, 0), ("Y", 0, 1), ("Z", 2, 1),
        ("Z", 0, 0), ("Z", 0, 1),
    ]


def send_order(S, C):
    if (S, C) != (4, 2):
        return [0, *range(C, min(2 * C, S * C)), *range(1, C), *range(2 * C, S * C)]
    return [0, 3, 4, 1, 2, 5, 7, 6]


def kernel(
    sizes,
    q_hbm, k_hbm, v_hbm, wo_hbm, wg_hbm, wu_hbm, wd_hbm, *rest
):
    S, H, C, T, F, D, E, A, B, R, parts, groups = sizes
    small = 12
    small_hbm, out_ref, rest = rest[:small], rest[small], rest[small + 1 :]
    small_ref, rest = rest[:small], rest[small:]
    (res_ref, mod_ref, router_ref, ids_ref, tile_ref, tile_t_ref,
     upper_ref, lower_ref, rowkey_ref, rowkey_t_ref, perm_ref, perm_t_ref) = small_ref
    P2 = len(parts)
    kbufs, rest = rest[:P2], rest[P2:]
    vbufs, rest = rest[:P2], rest[P2:]
    qbufs, rest = rest[:P2], rest[P2:]
    atts, rest = rest[:P2], rest[P2:]
    (hand, wo, wg, wu, wd,
     pbuf, prec, hidden, mixq,
     xout, xin, xs, yout, yrec, ysum, ret, placing, picks,
     ssem, lsem, wsem, kv_recv, kv_xsend, kv_zsend, q_send, q_recv, h_send, h_recv, a_send, a_recv,
     p_send, p_recv, d_send, d_recv, dx_send, y_send, y_recv, r_send, r_recv, result, osem) = rest
    N = S * C
    W = D // QUARTERS
    z, x, c = lax.axis_index("seq"), lax.axis_index("head"), lax.axis_index("cfg")
    me = z * C + c
    handing = any(p[2] for p in parts)

    small_loads = [pltpu.make_async_copy(a, b, ssem.at[i]) for i, (a, b) in enumerate(zip(small_hbm, small_ref))]
    for load in small_loads:
        load.start()

    def partner(d):
        return lax.rem(x + d, H)

    half = S // 2

    def near(n):
        if S % 2:
            return lax.rem(z + n, S)
        side = lax.rem(z // half + n % 2, 2)
        return side * half + lax.rem(lax.rem(z, half) + n // 2, half)

    def other(d):
        to_z, to_c = near(d // C), lax.rem(c + d % C, C)
        return to_z * C + to_c, {"seq": to_z, "cfg": to_c}

    def origin(d):
        return near(d // C) * C + lax.rem(c - d % C + C, C)

    def rows(i):
        return pl.ds(pl.multiple_of(i * T, T), T)

    def remote(src, dst, send, recv, device):
        return pltpu.make_async_remote_copy(
            src_ref=src, dst_ref=dst, send_sem=send, recv_sem=recv,
            device_id=device, device_id_type=MESH,
        )

    barrier = pltpu.get_barrier_semaphore()

    def greet(device):
        pl.semaphore_signal(barrier, inc=1, device_id=device, device_id_type=MESH)

    for d in range(1, H):
        greet({"head": partner(d)})
    for d in range(1, C):
        greet({"cfg": lax.rem(c + d, C)})
    for d in range(H):
        @pl.when(z < S - 1)
        def _():
            greet({"seq": z + 1, "head": partner(d)})

        @pl.when(z > 0)
        def _():
            greet({"seq": z - 1, "head": partner(d)})

    sides = jnp.where(z < S - 1, 1, 0) + jnp.where(z > 0, 1, 0)
    pl.semaphore_wait(barrier, H - 1 + C - 1 + H * sides)

    kv_src, kv_buf = (k_hbm, v_hbm), (kbufs, vbufs)
    outer = (z == 0) | (z == S - 1)
    inner = jnp.logical_not(outer)
    helping = (z == 1) | (z == S - 2)
    helper = jnp.where(z == 0, 1, S - 2)
    helped = jnp.where(z == 1, 0, S - 1)

    def cols(part, p):
        first, count, _ = parts[part]
        return pl.ds(pl.multiple_of(p * F + first * HEAD_DIM, 128), count * HEAD_DIM)

    def x_copy(kv, part, d):
        p = partner(d)
        return remote(
            kv_src[kv].at[:, cols(part, p)], kv_buf[kv][part].at[rows(x * S + z)],
            kv_xsend.at[kv, part, d - 1], kv_recv.at[kv, part, x * S + z], {"head": p},
        )

    def own_copy(kv, part):
        return pltpu.make_async_copy(
            kv_src[kv].at[:, cols(part, x)], kv_buf[kv][part].at[rows(x * S + z)], lsem.at[kv, part]
        )

    def z_copy(kv, part, ox, oz, step, own):
        block = ox * S + oz
        src = kv_src[kv].at[:, cols(part, x)] if own else kv_buf[kv][part].at[rows(block)]
        return remote(
            src, kv_buf[kv][part].at[rows(block)],
            kv_zsend.at[kv, part, block, 0 if step > 0 else 1], kv_recv.at[kv, part, block],
            {"seq": z + step},
        )

    def right(part):
        return z + 1 <= (S - 2 if parts[part][2] else S - 1)

    def leftward(part):
        return z - 1 >= (1 if parts[part][2] else 0)

    def both_ways(kv, part, ox, own, act):
        @pl.when(right(part))
        def _():
            act(z_copy(kv, part, ox, z, 1, own))

        @pl.when(leftward(part))
        def _():
            act(z_copy(kv, part, ox, z, -1, own))

    def q_copy(part, d):
        p = partner(d)
        return remote(
            q_hbm.at[:, cols(part, p)], qbufs[part].at[rows(x)],
            q_send.at[part, d - 1], q_recv.at[part, x], {"head": p},
        )

    def own_q(part):
        return pltpu.make_async_copy(q_hbm.at[:, cols(part, x)], qbufs[part].at[rows(x)], lsem.at[2, part])

    def hand_copy(d):
        p = partner(d)
        return remote(
            q_hbm.at[:, cols(0, p)], hand.at[rows(x)],
            h_send.at[d], h_recv.at[x], {"seq": helper, "head": p},
        )

    def give_back():
        return remote(hand, atts[0], a_send.at[0], a_recv.at[0], {"seq": helped})

    def q_start(part):
        if parts[part][2]:
            @pl.when(inner)
            def _():
                for d in range(1, H):
                    q_copy(part, d).start()
                own_q(part).start()

            @pl.when(outer)
            def _():
                for d in range(H):
                    hand_copy(d).start()
        else:
            for d in range(1, H):
                q_copy(part, d).start()
            own_q(part).start()

    def q_wait(part):
        own_q(part).wait()
        for d in range(1, H):
            p = partner(d)
            pltpu.make_async_copy(
                qbufs[part].at[rows(p)], qbufs[part].at[rows(p)], q_recv.at[part, p]
            ).wait()

    def begin(part):
        for kv in range(2):
            for d in range(1, H):
                x_copy(kv, part, d).start()
            both_ways(kv, part, x, True, lambda copy: copy.start())

    for part in range(P2):
        begin(part)
    for part in range(P2):
        q_start(part)
    for part in range(P2):
        for kv in range(2):
            own_copy(kv, part).start()
    loads = [
        pltpu.make_async_copy(a, b, wsem.at[i])
        for i, (a, b) in enumerate(((wo_hbm, wo), (wg_hbm.at[0], wg), (wu_hbm.at[0], wu), (wd_hbm.at[0], wd)))
    ]
    for load in loads:
        load.start()

    def arrived(kv, part, block):
        pltpu.make_async_copy(
            kv_buf[kv][part].at[rows(block)], kv_buf[kv][part].at[rows(block)], kv_recv.at[kv, part, block]
        ).wait()

    def relay(kv, part, j):
        if j == 0:
            for d in range(1, H):
                ox = partner(d)
                arrived(kv, part, ox * S + z)
                both_ways(kv, part, ox, False, lambda copy: copy.start())
            return
        low, high = (1, S - 2) if parts[part][2] else (0, S - 1)
        for d in range(H):
            ox = partner(d)

            @pl.when((z - j >= 0) & (z <= high))
            def _():
                arrived(kv, part, ox * S + z - j)

                @pl.when(z + 1 <= high)
                def _():
                    z_copy(kv, part, ox, z - j, 1, False).start()

            @pl.when((z + j < S) & (z >= low))
            def _():
                arrived(kv, part, ox * S + z + j)

                @pl.when(z - 1 >= low)
                def _():
                    z_copy(kv, part, ox, z + j, -1, False).start()

    for load in small_loads[3:10]:
        load.wait()
    ids = ids_ref[...].astype(F32).astype(BF16)
    ids_row = jnp.dot(ids, tile_ref[...], preferred_element_type=F32)
    ids_col = lax.dot_general(tile_t_ref[...], ids, (((1,), (1,)), ((), ())), preferred_element_type=F32)
    expert_rows = lax.broadcasted_iota(jnp.int32, (E, QUARTERS * T), 0).astype(F32)
    hot_row = [(ids_row[k : k + 1, :] == expert_rows).astype(F32) for k in range(2)]
    named = (hot_row[0] + hot_row[1])[:, :T].astype(BF16)
    earlier = jnp.dot(named, upper_ref[...], preferred_element_type=F32)
    slots = A + B
    quarter_row = (lax.broadcasted_iota(jnp.int32, (1, QUARTERS * T), 1) // T * (E * slots)).astype(F32)
    key_row = [
        quarter_row
        + ids_row[k : k + 1, :] * slots
        + jnp.sum(earlier * hot_row[k], axis=0, keepdims=True)
        for k in range(2)
    ]
    expert_cols = lax.broadcasted_iota(jnp.int32, (QUARTERS * T, E), 1).astype(F32)
    hot_col = [(ids_col[:, k : k + 1] == expert_cols).astype(F32) for k in range(2)]
    named = (hot_col[0] + hot_col[1])[:T, :].astype(BF16)
    earlier = jnp.dot(lower_ref[...], named, preferred_element_type=F32)
    quarter_col = (lax.broadcasted_iota(jnp.int32, (QUARTERS * T, 1), 0) // T * (E * slots)).astype(F32)
    key_col = [
        quarter_col
        + ids_col[:, k : k + 1] * slots
        + jnp.sum(earlier * hot_col[k], axis=1, keepdims=True)
        for k in range(2)
    ]

    placing[...] = (
        (rowkey_ref[...] == key_row[0]).astype(F32) + (rowkey_ref[...] == key_row[1]).astype(F32)
    ).astype(BF16)
    for k in range(2):
        picks[k] = (key_col[k] == rowkey_t_ref[...]).astype(BF16)

    heads = F // HEAD_DIM
    block_rows = H * T if H * T * H * S * T <= 131072 else T
    blocks = H * T // block_rows
    factor = HEAD_DIM ** (-0.5)

    def over_blocks(body):
        if blocks == 1:
            body(slice(0, block_rows))
        else:
            def step(i, carry):
                body(pl.ds(pl.multiple_of(i * block_rows, block_rows), block_rows))
                return carry

            lax.fori_loop(0, blocks, step, 0)


    def score(part, q, r, h):
        span = slice(h * HEAD_DIM, (h + 1) * HEAD_DIM)
        s = lax.dot_general(
            q[r, span], kbufs[part][:, span], (((1,), (1,)), ((), ())), preferred_element_type=F32,
        ) * factor
        w = jnp.exp(s - jnp.max(s, axis=1, keepdims=True))
        return w.astype(BF16), jnp.sum(w, axis=1, keepdims=True)

    def attend(part, q, out, r):
        for h in range(parts[part][1]):
            span = slice(h * HEAD_DIM, (h + 1) * HEAD_DIM)
            w, total = score(part, q, r, h)
            u = jnp.dot(w, vbufs[part][:, span], preferred_element_type=F32)
            out[r, span] = (u / total).astype(BF16)

    def attend_all(part, q, out):
        over_blocks(lambda r: attend(part, q, out, r))

    def early():
        own_copy(0, 0).wait()
        own_copy(1, 0).wait()
        if parts[0][2]:
            @pl.when(helping)
            def _():
                for d in range(H):
                    p = partner(d)
                    pltpu.make_async_copy(hand.at[rows(p)], hand.at[rows(p)], h_recv.at[p]).wait()
                attend_all(0, hand, hand)
                give_back().start()

            @pl.when(inner)
            def _():
                q_wait(0)
                attend_all(0, qbufs[0], atts[0])
        else:
            q_wait(0)
            attend_all(0, qbufs[0], atts[0])

    def step(j, among):
        for part in among:
            for kv in range(2):
                relay(kv, part, j)

    middle = S // 2 - 1 if P2 > 1 else S - 1
    for j in range(middle + 1):
        step(j, range(P2))
    for j in range(middle + 1, S):
        step(j, range(1))
    early()
    for part in range(1, P2):
        for j in range(middle + 1, S):
            step(j, (part,))
        own_copy(0, part).wait()
        own_copy(1, part).wait()
        q_wait(part)
    if handing:
        @pl.when(outer)
        def _():
            pltpu.make_async_copy(atts[0], atts[0], a_recv.at[0]).wait()

    for i, load in enumerate(small_loads):
        if not 3 <= i < 10:
            load.wait()
    loads[0].wait()

    step_rows = 16
    slices = T // step_rows

    def p_copy(d, i):
        p, s = partner(d), max(0, i - QUARTERS + 1)
        span = slice(i * W, (i + 1) * W) if i < QUARTERS else slice(0, D)
        return remote(
            pbuf.at[pl.ds(pl.multiple_of(p * T + s * step_rows, step_rows), step_rows), span],
            prec.at[d - 1, pl.ds(s * step_rows, step_rows), span],
            p_send.at[d - 1, i], p_recv.at[d - 1, i], {"head": p},
        )

    def project(p, span):
        pbuf[rows(p), span] = sum(
            jnp.dot(
                atts[part][rows(p), :],
                wo[parts[part][0] * HEAD_DIM : (parts[part][0] + parts[part][1]) * HEAD_DIM, span],
                preferred_element_type=F32,
            )
            for part in range(P2)
        ).astype(BF16)

    for d in [*range(1, H), 0]:
        p = partner(d)
        for part in range(1, P2):
            attend(part, qbufs[part], atts[part], rows(p))
        for i in range(QUARTERS):
            project(p, slice(i * W, (i + 1) * W))
            if d:
                p_copy(d, i).start()
        if d:
            for i in range(QUARTERS, QUARTERS + slices - 1):
                p_copy(d, i).start()

    def normalise(i):
        r = pl.ds(pl.multiple_of(i * step_rows, step_rows), step_rows)
        total = pbuf[pl.ds(pl.multiple_of(x * T + i * step_rows, step_rows), step_rows), :].astype(F32)
        for d in range(1, H):
            total = total + prec[d - 1, r, :].astype(F32)
        h = res_ref[0, r, :].astype(F32) + mod_ref[0, 0:1, :] * total
        hidden[r, :] = h
        centered = h - jnp.mean(h, axis=-1, keepdims=True)
        variance = jnp.mean(centered * centered, axis=-1, keepdims=True)
        mixed = (
            centered * lax.rsqrt(variance + EPSILON) * (1.0 + mod_ref[0, 2:3, :]) + mod_ref[0, 1:2, :]
        ).astype(BF16)
        for q in range(QUARTERS):
            mixq[pl.ds(pl.multiple_of(q * T + i * step_rows, step_rows), step_rows), :] = mixed[
                :, q * W : (q + 1) * W
            ]

    for s in range(slices):
        for d in range(1, H):
            for i in range(QUARTERS) if s == 0 else (QUARTERS + s - 1,):
                p_copy(d, i).wait_recv()
        normalise(s)

    def d_copy(d):
        o, device = other(d)
        return remote(xout.at[o], xin.at[x * N + me], d_send.at[d], d_recv.at[x * N + me], device)

    def dx_copy(d, o, own):
        p = partner(d)
        src = xout.at[me] if own else xin.at[x * N + o]
        return remote(src, xin.at[x * N + o], dx_send.at[d - 1, o], d_recv.at[x * N + o], {"head": p})

    def block_wait(buf, i, sem):
        pltpu.make_async_copy(buf.at[i], buf.at[i], sem).wait()

    own_x = pltpu.make_async_copy(xout.at[me], xin.at[x * N + me], lsem.at[2, 0])
    for d in send_order(S, C):
        o = other(d)[0]
        xout[o] = jnp.dot(
            placing[pl.ds(pl.multiple_of(o * R, 16), R), :], mixq[...], preferred_element_type=F32
        ).astype(BF16)
        if d:
            d_copy(d).start()
        else:
            for e in range(1, H):
                dx_copy(e, me, True).start()
            own_x.start()
    logits = sum(
        lax.dot_general(
            mixq[q * T : (q + 1) * T, :], router_ref[:, q * W : (q + 1) * W],
            (((1,), (1,)), ((), ())), preferred_element_type=F32,
        )
        for q in range(QUARTERS)
    )
    chosen = [jnp.sum(logits * hot_col[k][:T, :], axis=1, keepdims=True) for k in range(2)]
    gates = [jax.nn.sigmoid(chosen[0] - chosen[1]), jax.nn.sigmoid(chosen[1] - chosen[0])]
    def y_copy(d, o):
        p = partner(d)
        return remote(yout.at[p * N + o], yrec.at[d - 1, o], y_send.at[d - 1, o], y_recv.at[d - 1, o], {"head": p})

    def r_copy(d):
        o = origin(d)
        device = {"seq": o // C, "cfg": lax.rem(o, C)}
        return remote(ysum.at[o], ret.at[me], r_send.at[d], r_recv.at[me], device)

    def forward(d):
        if d == 0:
            own_x.wait()
            return
        o = origin(d)
        block_wait(xin, x * N + o, d_recv.at[x * N + o])
        for e in range(1, H):
            dx_copy(e, o, False).start()

    def y_start(d):
        for e in range(1, H):
            y_copy(e, origin(d)).start()

    size = N // groups

    def finish(d):
        o = origin(d)
        total = yout[x * N + o].astype(F32)
        for e in range(1, H):
            y_copy(e, o).wait_recv()
            total = total + yrec[e - 1, o].astype(F32)
        if d:
            ysum[o] = total.astype(BF16)
            r_copy(d).start()
        else:
            ret[me] = total.astype(BF16)

    g = perm_ref.shape[0] // (QUARTERS * B) if B else 1

    def mine(n):
        return list(range(n * size, (n + 1) * size))

    def expert(chosen):
        for e in range(1, H):
            for d in chosen:
                slot = partner(e) * N + origin(d)
                block_wait(xin, slot, d_recv.at[slot])
        places = [partner(e) * N + origin(d) for e in range(H) for d in chosen]
        for i, slot in enumerate(places):
            for q in range(QUARTERS):
                if A:
                    xs[q, i * A : (i + 1) * A, :] = xin[slot, q * A : (q + 1) * A, :]
        base = len(places) * A
        bundles = [(places[i : i + g] * g)[:g] for i in range(0, len(places), g)] if B else []
        for i, bundle in enumerate(bundles):
            mixed_b = jnp.concatenate([xin[slot, QUARTERS * A :, :] for slot in bundle], axis=0)
            mixed_b = jnp.dot(perm_ref[...], mixed_b, preferred_element_type=F32).astype(BF16)
            at = base + i * g * B
            for q in range(QUARTERS):
                xs[q, at : at + g * B, :] = mixed_b[q * g * B : (q + 1) * g * B, :]
        total = base + len(bundles) * g * B
        gate_out = sum(
            jnp.dot(xs[q, :total, :], wg[q * W : (q + 1) * W, :], preferred_element_type=F32)
            for q in range(QUARTERS)
        )
        up_out = sum(
            jnp.dot(xs[q, :total, :], wu[q * W : (q + 1) * W, :], preferred_element_type=F32)
            for q in range(QUARTERS)
        )
        activated = (gate_out / (1.0 + jnp.exp(-gate_out)) * up_out).astype(BF16)
        for q in range(QUARTERS):
            y = jnp.dot(activated, wd[:, q * W : (q + 1) * W], preferred_element_type=F32).astype(BF16)
            for i, slot in enumerate(places):
                if A:
                    yout[slot, q * A : (q + 1) * A, :] = y[i * A : (i + 1) * A, :]
            if B:
                xs[q, base:total, :] = y[base:, :]
        for i, bundle in enumerate(bundles):
            at = base + i * g * B
            mixed_b = jnp.concatenate([xs[q, at : at + g * B, :] for q in range(QUARTERS)], axis=0)
            mixed_b = jnp.dot(perm_t_ref[...], mixed_b, preferred_element_type=F32).astype(BF16)
            for k, slot in enumerate(places[i * g : (i + 1) * g]):
                yout[slot, QUARTERS * A :, :] = mixed_b[k * QUARTERS * B : (k + 1) * QUARTERS * B, :]

    for load in loads[1:]:
        load.wait()
    actions = {"F": forward, "Y": y_start, "Z": finish}
    for step, n, i in order(groups, size):
        if step == "D":
            expert(mine(n) if i < 0 else [n * size + i])
        else:
            actions[step](n * size + i)
    for d in range(1, N):
        o = other(d)[0]
        block_wait(ret, o, r_recv.at[o])

    def out_copy(q):
        span = slice(q * W, (q + 1) * W)
        return pltpu.make_async_copy(result.at[:, span], out_ref.at[0, :, span], osem.at[q])

    back = ret[...].reshape(E * R, W)
    picked = [
        jnp.dot(picks[k], back, preferred_element_type=F32)
        for k in range(2)
    ]
    for q in range(QUARTERS):
        span = slice(q * W, (q + 1) * W)
        r = slice(q * T, (q + 1) * T)
        mix = gates[0] * picked[0][r, :] + gates[1] * picked[1][r, :]
        result[:, span] = (hidden[:, span] + mod_ref[0, 3:4, span] * mix).astype(BF16)
        out_copy(q).start()
    for q in range(QUARTERS):
        out_copy(q).wait()

    for part in range(P2):
        low, high = (1, S - 2) if parts[part][2] else (0, S - 1)
        for kv in range(2):
            for d in range(1, H):
                x_copy(kv, part, d).wait_send()
            for d in range(H):
                both_ways(kv, part, partner(d), d == 0, lambda copy: copy.wait_send())
            for j in range(1, S):
                for d in range(H):
                    ox = partner(d)

                    @pl.when((z - j >= 0) & (z + 1 <= high))
                    def _():
                        z_copy(kv, part, ox, z - j, 1, False).wait_send()

                    @pl.when((z + j < S) & (z - 1 >= low))
                    def _():
                        z_copy(kv, part, ox, z + j, -1, False).wait_send()
        if not parts[part][2]:
            for d in range(1, H):
                q_copy(part, d).wait_send()
    if handing:
        @pl.when(inner)
        def _():
            for d in range(1, H):
                q_copy(0, d).wait_send()

        @pl.when(outer)
        def _():
            for d in range(H):
                hand_copy(d).wait_send()

        @pl.when(helping)
        def _():
            give_back().wait_send()
    for d in range(1, H):
        for i in range(QUARTERS + slices - 1):
            p_copy(d, i).wait_send()
        dx_copy(d, me, True).wait_send()
        for o in range(N):
            y_copy(d, o).wait_send()
        for i in range(1, N):
            dx_copy(d, other(i)[0], False).wait_send()
    for d in range(1, N):
        d_copy(d).wait_send()
        r_copy(d).wait_send()


def solution(mesh):
    S, H, C = mesh.shape["seq"], mesh.shape["head"], mesh.shape["cfg"]
    N = S * C

    def local(
        residual, queries, key_rows, value_rows, out_weight, modulation, router,
        gate_weight, up_weight, down_weight, expert_ids,
    ):
        T, D = residual.shape[1:]
        F = queries.shape[2] // H
        E, FF = router.shape[1], gate_weight.shape[2]
        top = expert_ids.shape[2]
        capacity = max(2, (5 * top * T + 4 * E - 1) // (4 * E))
        A = capacity // 16 * 16
        B = -(-(capacity - A) // 4) * 4
        R, W, G = QUARTERS * (A + B), D // QUARTERS, H * N
        slots = A + B
        groups = 4 if S % 4 == 0 else 2 if S % 2 == 0 else 1
        group = G // groups
        key = np.zeros((E, R), np.float32)
        for e in range(E):
            for q in range(QUARTERS):
                first = q * E * slots + e * slots
                key[e, q * A : (q + 1) * A] = first + np.arange(A)
                at = QUARTERS * A + q * B
                key[e, at : at + B] = first + A + np.arange(B)
        key = key.reshape(E * R)
        upper = np.tile(np.triu(np.ones((T, T), np.float32), 1), (1, QUARTERS))
        perm = np.eye(8, dtype=np.float32)
        if B:
            g = max(n for n in range(1, group + 1) if group % n == 0 and n * QUARTERS * B <= 256)
            size = g * QUARTERS * B
            place = np.arange(size).reshape(g, QUARTERS, B).transpose(1, 0, 2).reshape(-1)
            perm = np.zeros((size, size), np.float32)
            perm[np.arange(size), place] = 1.0
        tiled = np.tile(np.eye(T, dtype=np.float32), (1, QUARTERS))
        heads = F // HEAD_DIM
        early = max(1, heads // 2) if heads > 1 else 0
        parts = ((0, early, S >= 4), (early, heads - early, False)) if early else ((0, heads, False),)
        widths = [count * HEAD_DIM for _, count, _ in parts]
        P2 = len(parts)
        sizes = (S, H, C, T, F, D, E, A, B, R, parts, groups)
        keys = H * S * T
        hbm, vmem = pl.BlockSpec(memory_space=pl.ANY), pl.BlockSpec(memory_space=pltpu.VMEM)
        dma = pltpu.SemaphoreType.DMA
        V = pltpu.VMEM
        small = (
            residual, modulation, router.T, expert_ids[0].T,
            jnp.asarray(tiled, BF16), jnp.asarray(tiled.T, BF16),
            jnp.asarray(upper, BF16), jnp.asarray(upper.T, BF16),
            jnp.asarray(key[:, None]), jnp.asarray(key[None, :]),
            jnp.asarray(perm, BF16), jnp.asarray(perm.T, BF16),
        )
        out = pl.pallas_call(
            functools.partial(kernel, sizes),
            out_shape=jax.ShapeDtypeStruct((1, T, D), BF16),
            in_specs=[hbm] * (7 + len(small)),
            out_specs=hbm,
            scratch_shapes=[
                *(V(a.shape, a.dtype) for a in small),
                *(V((keys, w), BF16) for w in widths), *(V((keys, w), BF16) for w in widths),
                *(V((H * T, w), BF16) for w in widths), *(V((H * T, w), BF16) for w in widths),
                V((H * T, widths[0]), BF16),
                V((F, D), BF16), V((D, FF), BF16), V((D, FF), BF16), V((FF, D), BF16),
                V((H * T, D), BF16), V((H - 1, T, D), BF16),
                V((T, D), F32), V((QUARTERS * T, W), BF16),
                V((E, R, W), BF16), V((G, R, W), BF16), V((QUARTERS, group * slots, W), BF16),
                V((G, R, W), BF16), V((H - 1, N, R, W), BF16),
                V((N, R, W), BF16), V((E, R, W), BF16),
                V((E * R, QUARTERS * T), BF16), V((2, QUARTERS * T, E * R), BF16),
                dma((len(small),)), dma((3, P2)), dma((4,)),
                dma((2, P2, H * S)), dma((2, P2, H - 1)), dma((2, P2, H * S, 2)),
                dma((P2, H - 1)), dma((P2, H)), dma((H,)), dma((H,)), dma((1,)), dma((1,)),
                dma((H - 1, QUARTERS + T // 16 - 1)), dma((H - 1, QUARTERS + T // 16 - 1)),
                dma((N,)), dma((G,)), dma((H - 1, N)), dma((H - 1, N)), dma((H - 1, N)),
                dma((N,)), dma((N,)), V((T, D), BF16), dma((QUARTERS,)),
            ],
            compiler_params=pltpu.CompilerParams(
                collective_id=0, has_side_effects=True, vmem_limit_bytes=63000 * 1024
            ),
        )(
            queries[0], key_rows[0], value_rows[0], out_weight, gate_weight, up_weight, down_weight, *small
        )
        return out

    rows = P("cfg", ("group", "seq", "head"), None)
    return jax.shard_map(
        local,
        mesh=mesh,
        in_specs=(
            rows, rows, rows, rows,
            P("head", None),
            P("cfg", "group", None),
            P(),
            P(("seq", "cfg"), None, "head"),
            P(("seq", "cfg"), None, "head"),
            P(("seq", "cfg"), "head", None),
            rows,
        ),
        out_specs=rows,
        check_vma=False,
    )
```

```python
import functools
import jax
import jax.numpy as jnp
import numpy as np
from jax import lax
from jax.experimental import pallas as pl
from jax.experimental.pallas import tpu as pltpu
from jax.sharding import PartitionSpec as P

HEAD_DIM = 128
EPSILON = 1e-06
QUARTERS = 4
MESH = pl.DeviceIdType.MESH
F32 = jnp.float32
BF16 = jnp.bfloat16


def order(groups, size):
    def every(step, n):
        return [(step, n, d) for d in range(size)]

    if groups == 1:
        return every("F", 0) + [("D", 0, -1)] + every("Y", 0) + every("Z", 0)
    if groups == 2:
        return (
            every("F", 0) + [("D", 0, -1)] + every("F", 1) + every("Y", 0) + [("D", 1, -1)]
            + every("Y", 1) + every("Z", 1) + every("Z", 0)
        )
    if size != 2:
        steps = every("F", 0) + every("F", 1) + every("F", 2) + every("F", 3)
        for n in (1, 2, 3, 0):
            steps += [("D", n, -1)] + every("Y", n)
        return steps + every("Z", 1) + every("Z", 2) + every("Z", 3) + every("Z", 0)
    return [
        ("F", 0, 1), ("F", 3, 1), ("F", 2, 0), ("F", 2, 1), ("F", 1, 1), ("D", 3, 1), ("Y", 3, 1),
        ("D", 2, 0), ("F", 3, 0), ("D", 1, 1), ("F", 0, 0), ("Y", 1, 1), ("F", 1, 0), ("Z", 3, 1),
        ("D", 3, 0), ("Z", 1, 1), ("Y", 3, 0), ("D", 2, 1), ("Y", 2, 1), ("D", 1, 0), ("Z", 3, 0),
        ("Y", 1, 0), ("D", 0, -1), ("Y", 2, 0), ("Z", 2, 1), ("Y", 0, 0), ("Z", 1, 0), ("Z", 2, 0),
        ("Y", 0, 1), ("Z", 0, 0), ("Z", 0, 1),
    ]


def send_order(S, C):
    if (S, C) != (4, 2):
        return [0, *range(C, min(2 * C, S * C)), *range(1, C), *range(2 * C, S * C)]
    return [0, 7, 1, 4, 5, 3, 6, 2]


def kernel(
    sizes,
    q_hbm, k_hbm, v_hbm, wo_hbm, wg_hbm, wu_hbm, wd_hbm, *rest
):
    S, H, C, T, F, D, E, A, B, R, parts, groups = sizes
    small = 12
    small_hbm, out_ref, rest = rest[:small], rest[small], rest[small + 1 :]
    small_ref, rest = rest[:small], rest[small:]
    (res_ref, mod_ref, router_ref, ids_ref, tile_ref, tile_t_ref,
     upper_ref, lower_ref, rowkey_ref, rowkey_t_ref, perm_ref, perm_t_ref) = small_ref
    P2 = len(parts)
    kbufs, rest = rest[:P2], rest[P2:]
    vbufs, rest = rest[:P2], rest[P2:]
    qbufs, rest = rest[:P2], rest[P2:]
    atts, rest = rest[:P2], rest[P2:]
    (hand, wo, wg, wu, wd,
     pbuf, prec, hidden, mixq,
     xout, xin, xs, yout, yrec, ysum, ret, placing, picks,
     ssem, lsem, wsem, kv_recv, kv_xsend, kv_zsend, q_send, q_recv, h_send, h_recv, a_send, a_recv,
     p_send, p_recv, d_send, d_recv, dx_send, y_send, y_recv, r_send, r_recv, result, osem) = rest
    N = S * C
    W = D // QUARTERS
    z, x, c = lax.axis_index("seq"), lax.axis_index("head"), lax.axis_index("cfg")
    me = z * C + c
    handing = any(p[2] for p in parts)

    small_loads = [pltpu.make_async_copy(a, b, ssem.at[i]) for i, (a, b) in enumerate(zip(small_hbm, small_ref))]
    for load in small_loads:
        load.start()

    def partner(d):
        return lax.rem(x + d, H)

    half = S // 2

    def near(n):
        if S % 2:
            return lax.rem(z + n, S)
        side = lax.rem(z // half + n % 2, 2)
        return side * half + lax.rem(lax.rem(z, half) + n // 2, half)

    def other(d):
        to_z, to_c = near(d // C), lax.rem(c + d % C, C)
        return to_z * C + to_c, {"seq": to_z, "cfg": to_c}

    def origin(d):
        return near(d // C) * C + lax.rem(c - d % C + C, C)

    def rows(i):
        return pl.ds(pl.multiple_of(i * T, T), T)

    def remote(src, dst, send, recv, device):
        return pltpu.make_async_remote_copy(
            src_ref=src, dst_ref=dst, send_sem=send, recv_sem=recv,
            device_id=device, device_id_type=MESH,
        )

    barrier = pltpu.get_barrier_semaphore()

    def greet(device):
        pl.semaphore_signal(barrier, inc=1, device_id=device, device_id_type=MESH)

    for d in range(1, H):
        greet({"head": partner(d)})
    for d in range(1, C):
        greet({"cfg": lax.rem(c + d, C)})
    for d in range(H):
        @pl.when(z < S - 1)
        def _():
            greet({"seq": z + 1, "head": partner(d)})

        @pl.when(z > 0)
        def _():
            greet({"seq": z - 1, "head": partner(d)})

    sides = jnp.where(z < S - 1, 1, 0) + jnp.where(z > 0, 1, 0)
    pl.semaphore_wait(barrier, H - 1 + C - 1 + H * sides)

    kv_src, kv_buf = (k_hbm, v_hbm), (kbufs, vbufs)
    outer = (z == 0) | (z == S - 1)
    inner = jnp.logical_not(outer)
    helping = (z == 1) | (z == S - 2)
    helper = jnp.where(z == 0, 1, S - 2)
    helped = jnp.where(z == 1, 0, S - 1)

    def cols(part, p):
        first, count, _ = parts[part]
        return pl.ds(pl.multiple_of(p * F + first * HEAD_DIM, 128), count * HEAD_DIM)

    def x_copy(kv, part, d):
        p = partner(d)
        return remote(
            kv_src[kv].at[:, cols(part, p)], kv_buf[kv][part].at[rows(x * S + z)],
            kv_xsend.at[kv, part, d - 1], kv_recv.at[kv, part, x * S + z], {"head": p},
        )

    def own_copy(kv, part):
        return pltpu.make_async_copy(
            kv_src[kv].at[:, cols(part, x)], kv_buf[kv][part].at[rows(x * S + z)], lsem.at[kv, part]
        )

    def z_copy(kv, part, ox, oz, step, own):
        block = ox * S + oz
        src = kv_src[kv].at[:, cols(part, x)] if own else kv_buf[kv][part].at[rows(block)]
        return remote(
            src, kv_buf[kv][part].at[rows(block)],
            kv_zsend.at[kv, part, block, 0 if step > 0 else 1], kv_recv.at[kv, part, block],
            {"seq": z + step},
        )

    def right(part):
        return z + 1 <= (S - 2 if parts[part][2] else S - 1)

    def leftward(part):
        return z - 1 >= (1 if parts[part][2] else 0)

    def both_ways(kv, part, ox, own, act):
        @pl.when(right(part))
        def _():
            act(z_copy(kv, part, ox, z, 1, own))

        @pl.when(leftward(part))
        def _():
            act(z_copy(kv, part, ox, z, -1, own))

    def q_copy(part, d):
        p = partner(d)
        return remote(
            q_hbm.at[:, cols(part, p)], qbufs[part].at[rows(x)],
            q_send.at[part, d - 1], q_recv.at[part, x], {"head": p},
        )

    def own_q(part):
        return pltpu.make_async_copy(q_hbm.at[:, cols(part, x)], qbufs[part].at[rows(x)], lsem.at[2, part])

    def hand_copy(d):
        p = partner(d)
        return remote(
            q_hbm.at[:, cols(0, p)], hand.at[rows(x)],
            h_send.at[d], h_recv.at[x], {"seq": helper, "head": p},
        )

    def give_back():
        return remote(hand, atts[0], a_send.at[0], a_recv.at[0], {"seq": helped})

    def q_start(part):
        if parts[part][2]:
            @pl.when(inner)
            def _():
                for d in range(1, H):
                    q_copy(part, d).start()
                own_q(part).start()

            @pl.when(outer)
            def _():
                for d in range(H):
                    hand_copy(d).start()
        else:
            for d in range(1, H):
                q_copy(part, d).start()
            own_q(part).start()

    def q_wait(part):
        own_q(part).wait()
        for d in range(1, H):
            p = partner(d)
            pltpu.make_async_copy(
                qbufs[part].at[rows(p)], qbufs[part].at[rows(p)], q_recv.at[part, p]
            ).wait()

    def begin(part):
        for kv in range(2):
            for d in range(1, H):
                x_copy(kv, part, d).start()
            both_ways(kv, part, x, True, lambda copy: copy.start())

    for part in range(P2):
        begin(part)
    for part in range(P2):
        q_start(part)
    for part in range(P2):
        for kv in range(2):
            own_copy(kv, part).start()
    loads = [
        pltpu.make_async_copy(a, b, wsem.at[i])
        for i, (a, b) in enumerate(((wo_hbm, wo), (wg_hbm.at[0], wg), (wu_hbm.at[0], wu), (wd_hbm.at[0], wd)))
    ]
    for load in loads:
        load.start()

    def arrived(kv, part, block):
        pltpu.make_async_copy(
            kv_buf[kv][part].at[rows(block)], kv_buf[kv][part].at[rows(block)], kv_recv.at[kv, part, block]
        ).wait()

    def relay(kv, part, j):
        if j == 0:
            for d in range(1, H):
                ox = partner(d)
                arrived(kv, part, ox * S + z)
                both_ways(kv, part, ox, False, lambda copy: copy.start())
            return
        low, high = (1, S - 2) if parts[part][2] else (0, S - 1)
        for d in range(H):
            ox = partner(d)

            @pl.when((z - j >= 0) & (z <= high))
            def _():
                arrived(kv, part, ox * S + z - j)

                @pl.when(z + 1 <= high)
                def _():
                    z_copy(kv, part, ox, z - j, 1, False).start()

            @pl.when((z + j < S) & (z >= low))
            def _():
                arrived(kv, part, ox * S + z + j)

                @pl.when(z - 1 >= low)
                def _():
                    z_copy(kv, part, ox, z + j, -1, False).start()

    for load in small_loads[3:10]:
        load.wait()
    ids = ids_ref[...].astype(F32).astype(BF16)
    ids_row = jnp.dot(ids, tile_ref[...], preferred_element_type=F32)
    ids_col = lax.dot_general(tile_t_ref[...], ids, (((1,), (1,)), ((), ())), preferred_element_type=F32)
    expert_rows = lax.broadcasted_iota(jnp.int32, (E, QUARTERS * T), 0).astype(F32)
    hot_row = [(ids_row[k : k + 1, :] == expert_rows).astype(F32) for k in range(2)]
    named = (hot_row[0] + hot_row[1])[:, :T].astype(BF16)
    earlier = jnp.dot(named, upper_ref[...], preferred_element_type=F32)
    slots = A + B
    quarter_row = (lax.broadcasted_iota(jnp.int32, (1, QUARTERS * T), 1) // T * (E * slots)).astype(F32)
    key_row = [
        quarter_row
        + ids_row[k : k + 1, :] * slots
        + jnp.sum(earlier * hot_row[k], axis=0, keepdims=True)
        for k in range(2)
    ]
    expert_cols = lax.broadcasted_iota(jnp.int32, (QUARTERS * T, E), 1).astype(F32)
    hot_col = [(ids_col[:, k : k + 1] == expert_cols).astype(F32) for k in range(2)]
    named = (hot_col[0] + hot_col[1])[:T, :].astype(BF16)
    earlier = jnp.dot(lower_ref[...], named, preferred_element_type=F32)
    quarter_col = (lax.broadcasted_iota(jnp.int32, (QUARTERS * T, 1), 0) // T * (E * slots)).astype(F32)
    key_col = [
        quarter_col
        + ids_col[:, k : k + 1] * slots
        + jnp.sum(earlier * hot_col[k], axis=1, keepdims=True)
        for k in range(2)
    ]

    placing[...] = (
        (rowkey_ref[...] == key_row[0]).astype(F32) + (rowkey_ref[...] == key_row[1]).astype(F32)
    ).astype(BF16)
    for k in range(2):
        picks[k] = (key_col[k] == rowkey_t_ref[...]).astype(BF16)

    heads = F // HEAD_DIM
    block_rows = H * T if H * T * H * S * T <= 131072 else T
    blocks = H * T // block_rows
    factor = HEAD_DIM ** (-0.5)

    def over_blocks(body):
        if blocks == 1:
            body(slice(0, block_rows))
        else:
            def step(i, carry):
                body(pl.ds(pl.multiple_of(i * block_rows, block_rows), block_rows))
                return carry

            lax.fori_loop(0, blocks, step, 0)


    def score(part, q, r, h):
        span = slice(h * HEAD_DIM, (h + 1) * HEAD_DIM)
        s = lax.dot_general(
            q[r, span], kbufs[part][:, span], (((1,), (1,)), ((), ())), preferred_element_type=F32,
        ) * factor
        w = jnp.exp(s - jnp.max(s, axis=1, keepdims=True))
        return w.astype(BF16), jnp.sum(w, axis=1, keepdims=True)

    def attend(part, q, out, r):
        for h in range(parts[part][1]):
            span = slice(h * HEAD_DIM, (h + 1) * HEAD_DIM)
            w, total = score(part, q, r, h)
            u = jnp.dot(w, vbufs[part][:, span], preferred_element_type=F32)
            out[r, span] = (u / total).astype(BF16)

    def attend_all(part, q, out):
        over_blocks(lambda r: attend(part, q, out, r))

    def early():
        own_copy(0, 0).wait()
        own_copy(1, 0).wait()
        if parts[0][2]:
            @pl.when(helping)
            def _():
                for d in range(H):
                    p = partner(d)
                    pltpu.make_async_copy(hand.at[rows(p)], hand.at[rows(p)], h_recv.at[p]).wait()
                attend_all(0, hand, hand)
                give_back().start()

            @pl.when(inner)
            def _():
                q_wait(0)
                attend_all(0, qbufs[0], atts[0])
        else:
            q_wait(0)
            attend_all(0, qbufs[0], atts[0])

    def step(j, among):
        for part in among:
            for kv in range(2):
                relay(kv, part, j)

    middle = S // 2 - 1 if P2 > 1 else S - 1
    for j in range(middle + 1):
        step(j, range(P2))
    for j in range(middle + 1, S):
        step(j, range(1))
    early()
    for part in range(1, P2):
        for j in range(middle + 1, S):
            step(j, (part,))
        own_copy(0, part).wait()
        own_copy(1, part).wait()
        q_wait(part)
    if handing:
        @pl.when(outer)
        def _():
            pltpu.make_async_copy(atts[0], atts[0], a_recv.at[0]).wait()

    for i, load in enumerate(small_loads):
        if not 3 <= i < 10:
            load.wait()
    loads[0].wait()

    step_rows = 16
    slices = T // step_rows

    def p_copy(d, i):
        p, s = partner(d), max(0, i - QUARTERS + 1)
        span = slice(i * W, (i + 1) * W) if i < QUARTERS else slice(0, D)
        return remote(
            pbuf.at[pl.ds(pl.multiple_of(p * T + s * step_rows, step_rows), step_rows), span],
            prec.at[d - 1, pl.ds(s * step_rows, step_rows), span],
            p_send.at[d - 1, i], p_recv.at[d - 1, i], {"head": p},
        )

    def project(p, span):
        pbuf[rows(p), span] = sum(
            jnp.dot(
                atts[part][rows(p), :],
                wo[parts[part][0] * HEAD_DIM : (parts[part][0] + parts[part][1]) * HEAD_DIM, span],
                preferred_element_type=F32,
            )
            for part in range(P2)
        ).astype(BF16)

    for d in [*range(1, H), 0]:
        p = partner(d)
        for part in range(1, P2):
            attend(part, qbufs[part], atts[part], rows(p))
        for i in range(QUARTERS):
            project(p, slice(i * W, (i + 1) * W))
            if d:
                p_copy(d, i).start()
        if d:
            for i in range(QUARTERS, QUARTERS + slices - 1):
                p_copy(d, i).start()

    def normalise(i):
        r = pl.ds(pl.multiple_of(i * step_rows, step_rows), step_rows)
        total = pbuf[pl.ds(pl.multiple_of(x * T + i * step_rows, step_rows), step_rows), :].astype(F32)
        for d in range(1, H):
            total = total + prec[d - 1, r, :].astype(F32)
        h = res_ref[0, r, :].astype(F32) + mod_ref[0, 0:1, :] * total
        hidden[r, :] = h
        centered = h - jnp.mean(h, axis=-1, keepdims=True)
        variance = jnp.mean(centered * centered, axis=-1, keepdims=True)
        mixed = (
            centered * lax.rsqrt(variance + EPSILON) * (1.0 + mod_ref[0, 2:3, :]) + mod_ref[0, 1:2, :]
        ).astype(BF16)
        for q in range(QUARTERS):
            mixq[pl.ds(pl.multiple_of(q * T + i * step_rows, step_rows), step_rows), :] = mixed[
                :, q * W : (q + 1) * W
            ]

    for s in range(slices):
        for d in range(1, H):
            for i in range(QUARTERS) if s == 0 else (QUARTERS + s - 1,):
                p_copy(d, i).wait_recv()
        normalise(s)

    def d_copy(d):
        o, device = other(d)
        return remote(xout.at[o], xin.at[x * N + me], d_send.at[d], d_recv.at[x * N + me], device)

    def dx_copy(d, o, own):
        p = partner(d)
        src = xout.at[me] if own else xin.at[x * N + o]
        return remote(src, xin.at[x * N + o], dx_send.at[d - 1, o], d_recv.at[x * N + o], {"head": p})

    def block_wait(buf, i, sem):
        pltpu.make_async_copy(buf.at[i], buf.at[i], sem).wait()

    own_x = pltpu.make_async_copy(xout.at[me], xin.at[x * N + me], lsem.at[2, 0])
    for d in send_order(S, C):
        o = other(d)[0]
        xout[o] = jnp.dot(
            placing[pl.ds(pl.multiple_of(o * R, 16), R), :], mixq[...], preferred_element_type=F32
        ).astype(BF16)
        if d:
            d_copy(d).start()
        else:
            for e in range(1, H):
                dx_copy(e, me, True).start()
            own_x.start()
    logits = sum(
        lax.dot_general(
            mixq[q * T : (q + 1) * T, :], router_ref[:, q * W : (q + 1) * W],
            (((1,), (1,)), ((), ())), preferred_element_type=F32,
        )
        for q in range(QUARTERS)
    )
    chosen = [jnp.sum(logits * hot_col[k][:T, :], axis=1, keepdims=True) for k in range(2)]
    gates = [jax.nn.sigmoid(chosen[0] - chosen[1]), jax.nn.sigmoid(chosen[1] - chosen[0])]
    def y_copy(d, o):
        p = partner(d)
        return remote(yout.at[p * N + o], yrec.at[d - 1, o], y_send.at[d - 1, o], y_recv.at[d - 1, o], {"head": p})

    def r_copy(d):
        o = origin(d)
        device = {"seq": o // C, "cfg": lax.rem(o, C)}
        return remote(ysum.at[o], ret.at[me], r_send.at[d], r_recv.at[me], device)

    def forward(d):
        if d == 0:
            own_x.wait()
            return
        o = origin(d)
        block_wait(xin, x * N + o, d_recv.at[x * N + o])
        for e in range(1, H):
            dx_copy(e, o, False).start()

    def y_start(d):
        for e in range(1, H):
            y_copy(e, origin(d)).start()

    size = N // groups

    def finish(d):
        o = origin(d)
        total = yout[x * N + o].astype(F32)
        for e in range(1, H):
            y_copy(e, o).wait_recv()
            total = total + yrec[e - 1, o].astype(F32)
        if d:
            ysum[o] = total.astype(BF16)
            r_copy(d).start()
        else:
            ret[me] = total.astype(BF16)

    g = perm_ref.shape[0] // (QUARTERS * B) if B else 1

    def mine(n):
        return list(range(n * size, (n + 1) * size))

    def expert(chosen):
        for e in range(1, H):
            for d in chosen:
                slot = partner(e) * N + origin(d)
                block_wait(xin, slot, d_recv.at[slot])
        places = [partner(e) * N + origin(d) for e in range(H) for d in chosen]
        for i, slot in enumerate(places):
            for q in range(QUARTERS):
                if A:
                    xs[q, i * A : (i + 1) * A, :] = xin[slot, q * A : (q + 1) * A, :]
        base = len(places) * A
        bundles = [(places[i : i + g] * g)[:g] for i in range(0, len(places), g)] if B else []
        for i, bundle in enumerate(bundles):
            mixed_b = jnp.concatenate([xin[slot, QUARTERS * A :, :] for slot in bundle], axis=0)
            mixed_b = jnp.dot(perm_ref[...], mixed_b, preferred_element_type=F32).astype(BF16)
            at = base + i * g * B
            for q in range(QUARTERS):
                xs[q, at : at + g * B, :] = mixed_b[q * g * B : (q + 1) * g * B, :]
        total = base + len(bundles) * g * B
        gate_out = sum(
            jnp.dot(xs[q, :total, :], wg[q * W : (q + 1) * W, :], preferred_element_type=F32)
            for q in range(QUARTERS)
        )
        up_out = sum(
            jnp.dot(xs[q, :total, :], wu[q * W : (q + 1) * W, :], preferred_element_type=F32)
            for q in range(QUARTERS)
        )
        activated = (gate_out / (1.0 + jnp.exp(-gate_out)) * up_out).astype(BF16)
        for q in range(QUARTERS):
            y = jnp.dot(activated, wd[:, q * W : (q + 1) * W], preferred_element_type=F32).astype(BF16)
            for i, slot in enumerate(places):
                if A:
                    yout[slot, q * A : (q + 1) * A, :] = y[i * A : (i + 1) * A, :]
            if B:
                xs[q, base:total, :] = y[base:, :]
        for i, bundle in enumerate(bundles):
            at = base + i * g * B
            mixed_b = jnp.concatenate([xs[q, at : at + g * B, :] for q in range(QUARTERS)], axis=0)
            mixed_b = jnp.dot(perm_t_ref[...], mixed_b, preferred_element_type=F32).astype(BF16)
            for k, slot in enumerate(places[i * g : (i + 1) * g]):
                yout[slot, QUARTERS * A :, :] = mixed_b[k * QUARTERS * B : (k + 1) * QUARTERS * B, :]

    for load in loads[1:]:
        load.wait()
    actions = {"F": forward, "Y": y_start, "Z": finish}
    for step, n, i in order(groups, size):
        if step == "D":
            expert(mine(n) if i < 0 else [n * size + i])
        else:
            actions[step](n * size + i)
    for d in range(1, N):
        o = other(d)[0]
        block_wait(ret, o, r_recv.at[o])

    def out_copy(q):
        span = slice(q * W, (q + 1) * W)
        return pltpu.make_async_copy(result.at[:, span], out_ref.at[0, :, span], osem.at[q])

    back = ret[...].reshape(E * R, W)
    picked = [
        jnp.dot(picks[k], back, preferred_element_type=F32)
        for k in range(2)
    ]
    for q in range(QUARTERS):
        span = slice(q * W, (q + 1) * W)
        r = slice(q * T, (q + 1) * T)
        mix = gates[0] * picked[0][r, :] + gates[1] * picked[1][r, :]
        result[:, span] = (hidden[:, span] + mod_ref[0, 3:4, span] * mix).astype(BF16)
        out_copy(q).start()
    for q in range(QUARTERS):
        out_copy(q).wait()

    for part in range(P2):
        low, high = (1, S - 2) if parts[part][2] else (0, S - 1)
        for kv in range(2):
            for d in range(1, H):
                x_copy(kv, part, d).wait_send()
            for d in range(H):
                both_ways(kv, part, partner(d), d == 0, lambda copy: copy.wait_send())
            for j in range(1, S):
                for d in range(H):
                    ox = partner(d)

                    @pl.when((z - j >= 0) & (z + 1 <= high))
                    def _():
                        z_copy(kv, part, ox, z - j, 1, False).wait_send()

                    @pl.when((z + j < S) & (z - 1 >= low))
                    def _():
                        z_copy(kv, part, ox, z + j, -1, False).wait_send()
        if not parts[part][2]:
            for d in range(1, H):
                q_copy(part, d).wait_send()
    if handing:
        @pl.when(inner)
        def _():
            for d in range(1, H):
                q_copy(0, d).wait_send()

        @pl.when(outer)
        def _():
            for d in range(H):
                hand_copy(d).wait_send()

        @pl.when(helping)
        def _():
            give_back().wait_send()
    for d in range(1, H):
        for i in range(QUARTERS + slices - 1):
            p_copy(d, i).wait_send()
        dx_copy(d, me, True).wait_send()
        for o in range(N):
            y_copy(d, o).wait_send()
        for i in range(1, N):
            dx_copy(d, other(i)[0], False).wait_send()
    for d in range(1, N):
        d_copy(d).wait_send()
        r_copy(d).wait_send()


def solution(mesh):
    S, H, C = mesh.shape["seq"], mesh.shape["head"], mesh.shape["cfg"]
    N = S * C

    def local(
        residual, queries, key_rows, value_rows, out_weight, modulation, router,
        gate_weight, up_weight, down_weight, expert_ids,
    ):
        T, D = residual.shape[1:]
        F = queries.shape[2] // H
        E, FF = router.shape[1], gate_weight.shape[2]
        top = expert_ids.shape[2]
        capacity = max(2, (5 * top * T + 4 * E - 1) // (4 * E))
        A = capacity // 16 * 16
        B = -(-(capacity - A) // 4) * 4
        R, W, G = QUARTERS * (A + B), D // QUARTERS, H * N
        slots = A + B
        groups = 4 if S % 4 == 0 else 2 if S % 2 == 0 else 1
        group = G // groups
        key = np.zeros((E, R), np.float32)
        for e in range(E):
            for q in range(QUARTERS):
                first = q * E * slots + e * slots
                key[e, q * A : (q + 1) * A] = first + np.arange(A)
                at = QUARTERS * A + q * B
                key[e, at : at + B] = first + A + np.arange(B)
        key = key.reshape(E * R)
        upper = np.tile(np.triu(np.ones((T, T), np.float32), 1), (1, QUARTERS))
        perm = np.eye(8, dtype=np.float32)
        if B:
            g = max(n for n in range(1, group + 1) if group % n == 0 and n * QUARTERS * B <= 256)
            size = g * QUARTERS * B
            place = np.arange(size).reshape(g, QUARTERS, B).transpose(1, 0, 2).reshape(-1)
            perm = np.zeros((size, size), np.float32)
            perm[np.arange(size), place] = 1.0
        tiled = np.tile(np.eye(T, dtype=np.float32), (1, QUARTERS))
        heads = F // HEAD_DIM
        early = max(1, heads // 2) if heads > 1 else 0
        parts = ((0, early, S >= 4), (early, heads - early, False)) if early else ((0, heads, False),)
        widths = [count * HEAD_DIM for _, count, _ in parts]
        P2 = len(parts)
        sizes = (S, H, C, T, F, D, E, A, B, R, parts, groups)
        keys = H * S * T
        hbm, vmem = pl.BlockSpec(memory_space=pl.ANY), pl.BlockSpec(memory_space=pltpu.VMEM)
        dma = pltpu.SemaphoreType.DMA
        V = pltpu.VMEM
        small = (
            residual, modulation, router.T, expert_ids[0].T,
            jnp.asarray(tiled, BF16), jnp.asarray(tiled.T, BF16),
            jnp.asarray(upper, BF16), jnp.asarray(upper.T, BF16),
            jnp.asarray(key[:, None]), jnp.asarray(key[None, :]),
            jnp.asarray(perm, BF16), jnp.asarray(perm.T, BF16),
        )
        out = pl.pallas_call(
            functools.partial(kernel, sizes),
            out_shape=jax.ShapeDtypeStruct((1, T, D), BF16),
            in_specs=[hbm] * (7 + len(small)),
            out_specs=hbm,
            scratch_shapes=[
                *(V(a.shape, a.dtype) for a in small),
                *(V((keys, w), BF16) for w in widths), *(V((keys, w), BF16) for w in widths),
                *(V((H * T, w), BF16) for w in widths), *(V((H * T, w), BF16) for w in widths),
                V((H * T, widths[0]), BF16),
                V((F, D), BF16), V((D, FF), BF16), V((D, FF), BF16), V((FF, D), BF16),
                V((H * T, D), BF16), V((H - 1, T, D), BF16),
                V((T, D), F32), V((QUARTERS * T, W), BF16),
                V((E, R, W), BF16), V((G, R, W), BF16), V((QUARTERS, group * slots, W), BF16),
                V((G, R, W), BF16), V((H - 1, N, R, W), BF16),
                V((N, R, W), BF16), V((E, R, W), BF16),
                V((E * R, QUARTERS * T), BF16), V((2, QUARTERS * T, E * R), BF16),
                dma((len(small),)), dma((3, P2)), dma((4,)),
                dma((2, P2, H * S)), dma((2, P2, H - 1)), dma((2, P2, H * S, 2)),
                dma((P2, H - 1)), dma((P2, H)), dma((H,)), dma((H,)), dma((1,)), dma((1,)),
                dma((H - 1, QUARTERS + T // 16 - 1)), dma((H - 1, QUARTERS + T // 16 - 1)),
                dma((N,)), dma((G,)), dma((H - 1, N)), dma((H - 1, N)), dma((H - 1, N)),
                dma((N,)), dma((N,)), V((T, D), BF16), dma((QUARTERS,)),
            ],
            compiler_params=pltpu.CompilerParams(
                collective_id=0, has_side_effects=True, vmem_limit_bytes=63000 * 1024
            ),
        )(
            queries[0], key_rows[0], value_rows[0], out_weight, gate_weight, up_weight, down_weight, *small
        )
        return out

    rows = P("cfg", ("group", "seq", "head"), None)
    return jax.shard_map(
        local,
        mesh=mesh,
        in_specs=(
            rows, rows, rows, rows,
            P("head", None),
            P("cfg", "group", None),
            P(),
            P(("seq", "cfg"), None, "head"),
            P(("seq", "cfg"), None, "head"),
            P(("seq", "cfg"), "head", None),
            rows,
        ),
        out_specs=rows,
        check_vma=False,
    )
```

```python
import functools
import jax
import jax.numpy as jnp
import numpy as np
from jax import lax
from jax.experimental import pallas as pl
from jax.experimental.pallas import tpu as pltpu
from jax.sharding import PartitionSpec as P

HEAD_DIM = 128
EPSILON = 1e-06
QUARTERS = 4
MESH = pl.DeviceIdType.MESH
F32 = jnp.float32
BF16 = jnp.bfloat16


def order(groups, size):
    def every(step, n):
        return [(step, n, d) for d in range(size)]

    if groups == 1:
        return every("F", 0) + [("D", 0, -1)] + every("Y", 0) + every("Z", 0)
    if groups == 2:
        return (
            every("F", 0) + [("D", 0, -1)] + every("F", 1) + every("Y", 0) + [("D", 1, -1)]
            + every("Y", 1) + every("Z", 1) + every("Z", 0)
        )
    if size != 2:
        steps = every("F", 0) + every("F", 1) + every("F", 2) + every("F", 3)
        for n in (1, 2, 3, 0):
            steps += [("D", n, -1)] + every("Y", n)
        return steps + every("Z", 1) + every("Z", 2) + every("Z", 3) + every("Z", 0)
    return [
        ("F", 0, 1), ("F", 3, 1), ("F", 2, 0), ("F", 2, 1), ("F", 1, 1), ("D", 3, 1), ("Y", 3, 1),
        ("D", 2, 0), ("F", 3, 0), ("D", 1, 1), ("F", 0, 0), ("Y", 1, 1), ("F", 1, 0), ("Z", 3, 1),
        ("D", 3, 0), ("Z", 1, 1), ("Y", 3, 0), ("D", 2, 1), ("Y", 2, 1), ("D", 1, 0), ("Z", 3, 0),
        ("Y", 1, 0), ("D", 0, -1), ("Y", 2, 0), ("Z", 2, 1), ("Y", 0, 0), ("Z", 1, 0), ("Z", 2, 0),
        ("Y", 0, 1), ("Z", 0, 0), ("Z", 0, 1),
    ]


def send_order(S, C):
    if (S, C) != (4, 2):
        return [0, *range(C, min(2 * C, S * C)), *range(1, C), *range(2 * C, S * C)]
    return [0, 7, 1, 4, 5, 3, 6, 2]


def kernel(
    sizes,
    q_hbm, k_hbm, v_hbm, wo_hbm, wg_hbm, wu_hbm, wd_hbm, *rest
):
    S, H, C, T, F, D, E, A, B, R, parts, groups = sizes
    small = 12
    small_hbm, out_ref, rest = rest[:small], rest[small], rest[small + 1 :]
    small_ref, rest = rest[:small], rest[small:]
    (res_ref, mod_ref, router_ref, ids_ref, tile_ref, tile_t_ref,
     upper_ref, lower_ref, rowkey_ref, rowkey_t_ref, perm_ref, perm_t_ref) = small_ref
    P2 = len(parts)
    kbufs, rest = rest[:P2], rest[P2:]
    vbufs, rest = rest[:P2], rest[P2:]
    qbufs, rest = rest[:P2], rest[P2:]
    atts, rest = rest[:P2], rest[P2:]
    (hand, wo, wg, wu, wd,
     pbuf, prec, hidden, mixq,
     xout, xin, xs, yout, yrec, ysum, ret, placing, picks,
     ssem, lsem, wsem, kv_recv, kv_xsend, kv_zsend, q_send, q_recv, h_send, h_recv, a_send, a_recv,
     p_send, p_recv, d_send, d_recv, dx_send, y_send, y_recv, r_send, r_recv, result, osem) = rest
    N = S * C
    W = D // QUARTERS
    z, x, c = lax.axis_index("seq"), lax.axis_index("head"), lax.axis_index("cfg")
    me = z * C + c
    handing = any(p[2] for p in parts)

    small_loads = [pltpu.make_async_copy(a, b, ssem.at[i]) for i, (a, b) in enumerate(zip(small_hbm, small_ref))]

    def partner(d):
        return lax.rem(x + d, H)

    half = S // 2

    def near(n):
        if S % 2:
            return lax.rem(z + n, S)
        side = lax.rem(z // half + n % 2, 2)
        return side * half + lax.rem(lax.rem(z, half) + n // 2, half)

    def other(d):
        to_z, to_c = near(d // C), lax.rem(c + d % C, C)
        return to_z * C + to_c, {"seq": to_z, "cfg": to_c}

    def origin(d):
        return near(d // C) * C + lax.rem(c - d % C + C, C)

    def rows(i):
        return pl.ds(pl.multiple_of(i * T, T), T)

    def remote(src, dst, send, recv, device):
        return pltpu.make_async_remote_copy(
            src_ref=src, dst_ref=dst, send_sem=send, recv_sem=recv,
            device_id=device, device_id_type=MESH,
        )

    barrier = pltpu.get_barrier_semaphore()

    def greet(device):
        pl.semaphore_signal(barrier, inc=1, device_id=device, device_id_type=MESH)

    for d in range(1, H):
        greet({"head": partner(d)})
    for d in range(1, C):
        greet({"cfg": lax.rem(c + d, C)})
    for d in range(H):
        @pl.when(z < S - 1)
        def _():
            greet({"seq": z + 1, "head": partner(d)})

        @pl.when(z > 0)
        def _():
            greet({"seq": z - 1, "head": partner(d)})

    sides = jnp.where(z < S - 1, 1, 0) + jnp.where(z > 0, 1, 0)
    for load in small_loads:
        load.start()
    pl.semaphore_wait(barrier, H - 1 + C - 1 + H * sides)

    kv_src, kv_buf = (k_hbm, v_hbm), (kbufs, vbufs)
    outer = (z == 0) | (z == S - 1)
    inner = jnp.logical_not(outer)
    helping = (z == 1) | (z == S - 2)
    helper = jnp.where(z == 0, 1, S - 2)
    helped = jnp.where(z == 1, 0, S - 1)

    def cols(part, p):
        first, count, _ = parts[part]
        return pl.ds(pl.multiple_of(p * F + first * HEAD_DIM, 128), count * HEAD_DIM)

    def x_copy(kv, part, d):
        p = partner(d)
        return remote(
            kv_src[kv].at[:, cols(part, p)], kv_buf[kv][part].at[rows(x * S + z)],
            kv_xsend.at[kv, part, d - 1], kv_recv.at[kv, part, x * S + z], {"head": p},
        )

    def own_copy(kv, part):
        return pltpu.make_async_copy(
            kv_src[kv].at[:, cols(part, x)], kv_buf[kv][part].at[rows(x * S + z)], lsem.at[kv, part]
        )

    def z_copy(kv, part, ox, oz, step, own):
        block = ox * S + oz
        src = kv_src[kv].at[:, cols(part, x)] if own else kv_buf[kv][part].at[rows(block)]
        return remote(
            src, kv_buf[kv][part].at[rows(block)],
            kv_zsend.at[kv, part, block, 0 if step > 0 else 1], kv_recv.at[kv, part, block],
            {"seq": z + step},
        )

    def right(part):
        return z + 1 <= (S - 2 if parts[part][2] else S - 1)

    def leftward(part):
        return z - 1 >= (1 if parts[part][2] else 0)

    def both_ways(kv, part, ox, own, act):
        @pl.when(right(part))
        def _():
            act(z_copy(kv, part, ox, z, 1, own))

        @pl.when(leftward(part))
        def _():
            act(z_copy(kv, part, ox, z, -1, own))

    def q_copy(part, d):
        p = partner(d)
        return remote(
            q_hbm.at[:, cols(part, p)], qbufs[part].at[rows(x)],
            q_send.at[part, d - 1], q_recv.at[part, x], {"head": p},
        )

    def own_q(part):
        return pltpu.make_async_copy(q_hbm.at[:, cols(part, x)], qbufs[part].at[rows(x)], lsem.at[2, part])

    def hand_copy(d):
        p = partner(d)
        return remote(
            q_hbm.at[:, cols(0, p)], hand.at[rows(x)],
            h_send.at[d], h_recv.at[x], {"seq": helper, "head": p},
        )

    def give_back():
        return remote(hand, atts[0], a_send.at[0], a_recv.at[0], {"seq": helped})

    def q_start(part):
        if parts[part][2]:
            @pl.when(inner)
            def _():
                for d in range(1, H):
                    q_copy(part, d).start()
                own_q(part).start()

            @pl.when(outer)
            def _():
                for d in range(H):
                    hand_copy(d).start()
        else:
            for d in range(1, H):
                q_copy(part, d).start()
            own_q(part).start()

    def q_wait(part):
        own_q(part).wait()
        for d in range(1, H):
            p = partner(d)
            pltpu.make_async_copy(
                qbufs[part].at[rows(p)], qbufs[part].at[rows(p)], q_recv.at[part, p]
            ).wait()

    def begin(part):
        for kv in range(2):
            for d in range(1, H):
                x_copy(kv, part, d).start()
            both_ways(kv, part, x, True, lambda copy: copy.start())

    for part in range(P2):
        begin(part)
    for part in range(P2):
        q_start(part)
    for part in range(P2):
        for kv in range(2):
            own_copy(kv, part).start()
    loads = [
        pltpu.make_async_copy(a, b, wsem.at[i])
        for i, (a, b) in enumerate(((wo_hbm, wo), (wg_hbm.at[0], wg), (wu_hbm.at[0], wu), (wd_hbm.at[0], wd)))
    ]
    for load in loads:
        load.start()

    def arrived(kv, part, block):
        pltpu.make_async_copy(
            kv_buf[kv][part].at[rows(block)], kv_buf[kv][part].at[rows(block)], kv_recv.at[kv, part, block]
        ).wait()

    def relay(kv, part, j):
        if j == 0:
            for d in range(1, H):
                ox = partner(d)
                arrived(kv, part, ox * S + z)
                both_ways(kv, part, ox, False, lambda copy: copy.start())
            return
        low, high = (1, S - 2) if parts[part][2] else (0, S - 1)
        for d in range(H):
            ox = partner(d)

            @pl.when((z - j >= 0) & (z <= high))
            def _():
                arrived(kv, part, ox * S + z - j)

                @pl.when(z + 1 <= high)
                def _():
                    z_copy(kv, part, ox, z - j, 1, False).start()

            @pl.when((z + j < S) & (z >= low))
            def _():
                arrived(kv, part, ox * S + z + j)

                @pl.when(z - 1 >= low)
                def _():
                    z_copy(kv, part, ox, z + j, -1, False).start()

    for load in small_loads[3:10]:
        load.wait()
    ids = ids_ref[...].astype(F32).astype(BF16)
    ids_row = jnp.dot(ids, tile_ref[...], preferred_element_type=F32)
    ids_col = lax.dot_general(tile_t_ref[...], ids, (((1,), (1,)), ((), ())), preferred_element_type=F32)
    expert_rows = lax.broadcasted_iota(jnp.int32, (E, QUARTERS * T), 0).astype(F32)
    hot_row = [(ids_row[k : k + 1, :] == expert_rows).astype(F32) for k in range(2)]
    named = (hot_row[0] + hot_row[1])[:, :T].astype(BF16)
    earlier = jnp.dot(named, upper_ref[...], preferred_element_type=F32)
    slots = A + B
    quarter_row = (lax.broadcasted_iota(jnp.int32, (1, QUARTERS * T), 1) // T * (E * slots)).astype(F32)
    key_row = [
        quarter_row
        + ids_row[k : k + 1, :] * slots
        + jnp.sum(earlier * hot_row[k], axis=0, keepdims=True)
        for k in range(2)
    ]
    expert_cols = lax.broadcasted_iota(jnp.int32, (QUARTERS * T, E), 1).astype(F32)
    hot_col = [(ids_col[:, k : k + 1] == expert_cols).astype(F32) for k in range(2)]
    named = (hot_col[0] + hot_col[1])[:T, :].astype(BF16)
    earlier = jnp.dot(lower_ref[...], named, preferred_element_type=F32)
    quarter_col = (lax.broadcasted_iota(jnp.int32, (QUARTERS * T, 1), 0) // T * (E * slots)).astype(F32)
    key_col = [
        quarter_col
        + ids_col[:, k : k + 1] * slots
        + jnp.sum(earlier * hot_col[k], axis=1, keepdims=True)
        for k in range(2)
    ]

    placing[...] = (
        (rowkey_ref[...] == key_row[0]).astype(F32) + (rowkey_ref[...] == key_row[1]).astype(F32)
    ).astype(BF16)
    for k in range(2):
        picks[k] = (key_col[k] == rowkey_t_ref[...]).astype(BF16)

    heads = F // HEAD_DIM
    block_rows = H * T if H * T * H * S * T <= 131072 else T
    blocks = H * T // block_rows
    factor = HEAD_DIM ** (-0.5)

    def over_blocks(body):
        if blocks == 1:
            body(slice(0, block_rows))
        else:
            def step(i, carry):
                body(pl.ds(pl.multiple_of(i * block_rows, block_rows), block_rows))
                return carry

            lax.fori_loop(0, blocks, step, 0)


    def score(part, q, r, h):
        span = slice(h * HEAD_DIM, (h + 1) * HEAD_DIM)
        s = lax.dot_general(
            q[r, span], kbufs[part][:, span], (((1,), (1,)), ((), ())), preferred_element_type=F32,
        ) * factor
        w = jnp.exp(s - jnp.max(s, axis=1, keepdims=True))
        return w.astype(BF16), jnp.sum(w, axis=1, keepdims=True)

    def attend(part, q, out, r):
        for h in range(parts[part][1]):
            span = slice(h * HEAD_DIM, (h + 1) * HEAD_DIM)
            w, total = score(part, q, r, h)
            u = jnp.dot(w, vbufs[part][:, span], preferred_element_type=F32)
            out[r, span] = (u / total).astype(BF16)

    def attend_all(part, q, out):
        over_blocks(lambda r: attend(part, q, out, r))

    def early():
        own_copy(0, 0).wait()
        own_copy(1, 0).wait()
        if parts[0][2]:
            @pl.when(helping)
            def _():
                for d in range(H):
                    p = partner(d)
                    pltpu.make_async_copy(hand.at[rows(p)], hand.at[rows(p)], h_recv.at[p]).wait()
                attend_all(0, hand, hand)
                give_back().start()

            @pl.when(inner)
            def _():
                q_wait(0)
                attend_all(0, qbufs[0], atts[0])
        else:
            q_wait(0)
            attend_all(0, qbufs[0], atts[0])

    def step(j, among):
        for part in among:
            for kv in range(2):
                relay(kv, part, j)

    middle = S // 2 - 1 if P2 > 1 else S - 1
    for j in range(middle + 1):
        step(j, range(P2))
    for j in range(middle + 1, S):
        step(j, range(1))
    early()
    for part in range(1, P2):
        for j in range(middle + 1, S):
            step(j, (part,))
        own_copy(0, part).wait()
        own_copy(1, part).wait()
        q_wait(part)
    if handing:
        @pl.when(outer)
        def _():
            pltpu.make_async_copy(atts[0], atts[0], a_recv.at[0]).wait()

    for i, load in enumerate(small_loads):
        if not 3 <= i < 10:
            load.wait()
    loads[0].wait()

    step_rows = 16
    slices = T // step_rows

    def p_copy(d, i):
        p, s = partner(d), max(0, i - QUARTERS + 1)
        span = slice(i * W, (i + 1) * W) if i < QUARTERS else slice(0, D)
        return remote(
            pbuf.at[pl.ds(pl.multiple_of(p * T + s * step_rows, step_rows), step_rows), span],
            prec.at[d - 1, pl.ds(s * step_rows, step_rows), span],
            p_send.at[d - 1, i], p_recv.at[d - 1, i], {"head": p},
        )

    def project(p, span):
        pbuf[rows(p), span] = sum(
            jnp.dot(
                atts[part][rows(p), :],
                wo[parts[part][0] * HEAD_DIM : (parts[part][0] + parts[part][1]) * HEAD_DIM, span],
                preferred_element_type=F32,
            )
            for part in range(P2)
        ).astype(BF16)

    for d in [*range(1, H), 0]:
        p = partner(d)
        for part in range(1, P2):
            attend(part, qbufs[part], atts[part], rows(p))
        for i in range(QUARTERS):
            project(p, slice(i * W, (i + 1) * W))
            if d:
                p_copy(d, i).start()
        if d:
            for i in range(QUARTERS, QUARTERS + slices - 1):
                p_copy(d, i).start()

    def normalise(i):
        r = pl.ds(pl.multiple_of(i * step_rows, step_rows), step_rows)
        total = pbuf[pl.ds(pl.multiple_of(x * T + i * step_rows, step_rows), step_rows), :].astype(F32)
        for d in range(1, H):
            total = total + prec[d - 1, r, :].astype(F32)
        h = res_ref[0, r, :].astype(F32) + mod_ref[0, 0:1, :] * total
        hidden[r, :] = h
        centered = h - jnp.mean(h, axis=-1, keepdims=True)
        variance = jnp.mean(centered * centered, axis=-1, keepdims=True)
        mixed = (
            centered * lax.rsqrt(variance + EPSILON) * (1.0 + mod_ref[0, 2:3, :]) + mod_ref[0, 1:2, :]
        ).astype(BF16)
        for q in range(QUARTERS):
            mixq[pl.ds(pl.multiple_of(q * T + i * step_rows, step_rows), step_rows), :] = mixed[
                :, q * W : (q + 1) * W
            ]

    for s in range(slices):
        for d in range(1, H):
            for i in range(QUARTERS) if s == 0 else (QUARTERS + s - 1,):
                p_copy(d, i).wait_recv()
        normalise(s)

    def d_copy(d):
        o, device = other(d)
        return remote(xout.at[o], xin.at[x * N + me], d_send.at[d], d_recv.at[x * N + me], device)

    def dx_copy(d, o, own):
        p = partner(d)
        src = xout.at[me] if own else xin.at[x * N + o]
        return remote(src, xin.at[x * N + o], dx_send.at[d - 1, o], d_recv.at[x * N + o], {"head": p})

    def block_wait(buf, i, sem):
        pltpu.make_async_copy(buf.at[i], buf.at[i], sem).wait()

    own_x = pltpu.make_async_copy(xout.at[me], xin.at[x * N + me], lsem.at[2, 0])
    for d in send_order(S, C):
        o = other(d)[0]
        xout[o] = jnp.dot(
            placing[pl.ds(pl.multiple_of(o * R, 16), R), :], mixq[...], preferred_element_type=F32
        ).astype(BF16)
        if d:
            d_copy(d).start()
        else:
            for e in range(1, H):
                dx_copy(e, me, True).start()
            own_x.start()
    logits = sum(
        lax.dot_general(
            mixq[q * T : (q + 1) * T, :], router_ref[:, q * W : (q + 1) * W],
            (((1,), (1,)), ((), ())), preferred_element_type=F32,
        )
        for q in range(QUARTERS)
    )
    chosen = [jnp.sum(logits * hot_col[k][:T, :], axis=1, keepdims=True) for k in range(2)]
    gates = [jax.nn.sigmoid(chosen[0] - chosen[1]), jax.nn.sigmoid(chosen[1] - chosen[0])]
    def y_copy(d, o):
        p = partner(d)
        return remote(yout.at[p * N + o], yrec.at[d - 1, o], y_send.at[d - 1, o], y_recv.at[d - 1, o], {"head": p})

    def r_copy(d):
        o = origin(d)
        device = {"seq": o // C, "cfg": lax.rem(o, C)}
        return remote(ysum.at[o], ret.at[me], r_send.at[d], r_recv.at[me], device)

    def forward(d):
        if d == 0:
            own_x.wait()
            return
        o = origin(d)
        block_wait(xin, x * N + o, d_recv.at[x * N + o])
        for e in range(1, H):
            dx_copy(e, o, False).start()

    def y_start(d):
        for e in range(1, H):
            y_copy(e, origin(d)).start()

    size = N // groups

    def finish(d):
        o = origin(d)
        total = yout[x * N + o].astype(F32)
        for e in range(1, H):
            y_copy(e, o).wait_recv()
            total = total + yrec[e - 1, o].astype(F32)
        if d:
            ysum[o] = total.astype(BF16)
            r_copy(d).start()
        else:
            ret[me] = total.astype(BF16)

    g = perm_ref.shape[0] // (QUARTERS * B) if B else 1

    def mine(n):
        return list(range(n * size, (n + 1) * size))

    def expert(chosen):
        for e in range(1, H):
            for d in chosen:
                slot = partner(e) * N + origin(d)
                block_wait(xin, slot, d_recv.at[slot])
        places = [partner(e) * N + origin(d) for e in range(H) for d in chosen]
        for i, slot in enumerate(places):
            for q in range(QUARTERS):
                if A:
                    xs[q, i * A : (i + 1) * A, :] = xin[slot, q * A : (q + 1) * A, :]
        base = len(places) * A
        bundles = [(places[i : i + g] * g)[:g] for i in range(0, len(places), g)] if B else []
        for i, bundle in enumerate(bundles):
            mixed_b = jnp.concatenate([xin[slot, QUARTERS * A :, :] for slot in bundle], axis=0)
            mixed_b = jnp.dot(perm_ref[...], mixed_b, preferred_element_type=F32).astype(BF16)
            at = base + i * g * B
            for q in range(QUARTERS):
                xs[q, at : at + g * B, :] = mixed_b[q * g * B : (q + 1) * g * B, :]
        total = base + len(bundles) * g * B
        gate_out = sum(
            jnp.dot(xs[q, :total, :], wg[q * W : (q + 1) * W, :], preferred_element_type=F32)
            for q in range(QUARTERS)
        )
        up_out = sum(
            jnp.dot(xs[q, :total, :], wu[q * W : (q + 1) * W, :], preferred_element_type=F32)
            for q in range(QUARTERS)
        )
        activated = (gate_out / (1.0 + jnp.exp(-gate_out)) * up_out).astype(BF16)
        for q in range(QUARTERS):
            y = jnp.dot(activated, wd[:, q * W : (q + 1) * W], preferred_element_type=F32).astype(BF16)
            for i, slot in enumerate(places):
                if A:
                    yout[slot, q * A : (q + 1) * A, :] = y[i * A : (i + 1) * A, :]
            if B:
                xs[q, base:total, :] = y[base:, :]
        for i, bundle in enumerate(bundles):
            at = base + i * g * B
            mixed_b = jnp.concatenate([xs[q, at : at + g * B, :] for q in range(QUARTERS)], axis=0)
            mixed_b = jnp.dot(perm_t_ref[...], mixed_b, preferred_element_type=F32).astype(BF16)
            for k, slot in enumerate(places[i * g : (i + 1) * g]):
                yout[slot, QUARTERS * A :, :] = mixed_b[k * QUARTERS * B : (k + 1) * QUARTERS * B, :]

    for load in loads[1:]:
        load.wait()
    actions = {"F": forward, "Y": y_start, "Z": finish}
    for step, n, i in order(groups, size):
        if step == "D":
            expert(mine(n) if i < 0 else [n * size + i])
        else:
            actions[step](n * size + i)
    for d in range(1, N):
        o = other(d)[0]
        block_wait(ret, o, r_recv.at[o])

    def out_copy(q):
        span = slice(q * W, (q + 1) * W)
        return pltpu.make_async_copy(result.at[:, span], out_ref.at[0, :, span], osem.at[q])

    back = ret[...].reshape(E * R, W)
    picked = [
        jnp.dot(picks[k], back, preferred_element_type=F32)
        for k in range(2)
    ]
    for q in range(QUARTERS):
        span = slice(q * W, (q + 1) * W)
        r = slice(q * T, (q + 1) * T)
        mix = gates[0] * picked[0][r, :] + gates[1] * picked[1][r, :]
        result[:, span] = (hidden[:, span] + mod_ref[0, 3:4, span] * mix).astype(BF16)
        out_copy(q).start()
    for q in range(QUARTERS):
        out_copy(q).wait()

    for part in range(P2):
        low, high = (1, S - 2) if parts[part][2] else (0, S - 1)
        for kv in range(2):
            for d in range(1, H):
                x_copy(kv, part, d).wait_send()
            for d in range(H):
                both_ways(kv, part, partner(d), d == 0, lambda copy: copy.wait_send())
            for j in range(1, S):
                for d in range(H):
                    ox = partner(d)

                    @pl.when((z - j >= 0) & (z + 1 <= high))
                    def _():
                        z_copy(kv, part, ox, z - j, 1, False).wait_send()

                    @pl.when((z + j < S) & (z - 1 >= low))
                    def _():
                        z_copy(kv, part, ox, z + j, -1, False).wait_send()
        if not parts[part][2]:
            for d in range(1, H):
                q_copy(part, d).wait_send()
    if handing:
        @pl.when(inner)
        def _():
            for d in range(1, H):
                q_copy(0, d).wait_send()

        @pl.when(outer)
        def _():
            for d in range(H):
                hand_copy(d).wait_send()

        @pl.when(helping)
        def _():
            give_back().wait_send()
    for d in range(1, H):
        for i in range(QUARTERS + slices - 1):
            p_copy(d, i).wait_send()
        dx_copy(d, me, True).wait_send()
        for o in range(N):
            y_copy(d, o).wait_send()
        for i in range(1, N):
            dx_copy(d, other(i)[0], False).wait_send()
    for d in range(1, N):
        d_copy(d).wait_send()
        r_copy(d).wait_send()


def solution(mesh):
    S, H, C = mesh.shape["seq"], mesh.shape["head"], mesh.shape["cfg"]
    N = S * C

    def local(
        residual, queries, key_rows, value_rows, out_weight, modulation, router,
        gate_weight, up_weight, down_weight, expert_ids,
    ):
        T, D = residual.shape[1:]
        F = queries.shape[2] // H
        E, FF = router.shape[1], gate_weight.shape[2]
        top = expert_ids.shape[2]
        capacity = max(2, (5 * top * T + 4 * E - 1) // (4 * E))
        A = capacity // 16 * 16
        B = -(-(capacity - A) // 4) * 4
        R, W, G = QUARTERS * (A + B), D // QUARTERS, H * N
        slots = A + B
        groups = 4 if S % 4 == 0 else 2 if S % 2 == 0 else 1
        group = G // groups
        key = np.zeros((E, R), np.float32)
        for e in range(E):
            for q in range(QUARTERS):
                first = q * E * slots + e * slots
                key[e, q * A : (q + 1) * A] = first + np.arange(A)
                at = QUARTERS * A + q * B
                key[e, at : at + B] = first + A + np.arange(B)
        key = key.reshape(E * R)
        upper = np.tile(np.triu(np.ones((T, T), np.float32), 1), (1, QUARTERS))
        perm = np.eye(8, dtype=np.float32)
        if B:
            g = max(n for n in range(1, group + 1) if group % n == 0 and n * QUARTERS * B <= 256)
            size = g * QUARTERS * B
            place = np.arange(size).reshape(g, QUARTERS, B).transpose(1, 0, 2).reshape(-1)
            perm = np.zeros((size, size), np.float32)
            perm[np.arange(size), place] = 1.0
        tiled = np.tile(np.eye(T, dtype=np.float32), (1, QUARTERS))
        heads = F // HEAD_DIM
        early = max(1, heads // 2) if heads > 1 else 0
        parts = ((0, early, S >= 4), (early, heads - early, False)) if early else ((0, heads, False),)
        widths = [count * HEAD_DIM for _, count, _ in parts]
        P2 = len(parts)
        sizes = (S, H, C, T, F, D, E, A, B, R, parts, groups)
        keys = H * S * T
        hbm, vmem = pl.BlockSpec(memory_space=pl.ANY), pl.BlockSpec(memory_space=pltpu.VMEM)
        dma = pltpu.SemaphoreType.DMA
        V = pltpu.VMEM
        small = (
            residual, modulation, router.T, expert_ids[0].T,
            jnp.asarray(tiled, BF16), jnp.asarray(tiled.T, BF16),
            jnp.asarray(upper, BF16), jnp.asarray(upper.T, BF16),
            jnp.asarray(key[:, None]), jnp.asarray(key[None, :]),
            jnp.asarray(perm, BF16), jnp.asarray(perm.T, BF16),
        )
        out = pl.pallas_call(
            functools.partial(kernel, sizes),
            out_shape=jax.ShapeDtypeStruct((1, T, D), BF16),
            in_specs=[hbm] * (7 + len(small)),
            out_specs=hbm,
            scratch_shapes=[
                *(V(a.shape, a.dtype) for a in small),
                *(V((keys, w), BF16) for w in widths), *(V((keys, w), BF16) for w in widths),
                *(V((H * T, w), BF16) for w in widths), *(V((H * T, w), BF16) for w in widths),
                V((H * T, widths[0]), BF16),
                V((F, D), BF16), V((D, FF), BF16), V((D, FF), BF16), V((FF, D), BF16),
                V((H * T, D), BF16), V((H - 1, T, D), BF16),
                V((T, D), F32), V((QUARTERS * T, W), BF16),
                V((E, R, W), BF16), V((G, R, W), BF16), V((QUARTERS, group * slots, W), BF16),
                V((G, R, W), BF16), V((H - 1, N, R, W), BF16),
                V((N, R, W), BF16), V((E, R, W), BF16),
                V((E * R, QUARTERS * T), BF16), V((2, QUARTERS * T, E * R), BF16),
                dma((len(small),)), dma((3, P2)), dma((4,)),
                dma((2, P2, H * S)), dma((2, P2, H - 1)), dma((2, P2, H * S, 2)),
                dma((P2, H - 1)), dma((P2, H)), dma((H,)), dma((H,)), dma((1,)), dma((1,)),
                dma((H - 1, QUARTERS + T // 16 - 1)), dma((H - 1, QUARTERS + T // 16 - 1)),
                dma((N,)), dma((G,)), dma((H - 1, N)), dma((H - 1, N)), dma((H - 1, N)),
                dma((N,)), dma((N,)), V((T, D), BF16), dma((QUARTERS,)),
            ],
            compiler_params=pltpu.CompilerParams(
                collective_id=0, has_side_effects=True, vmem_limit_bytes=63000 * 1024
            ),
        )(
            queries[0], key_rows[0], value_rows[0], out_weight, gate_weight, up_weight, down_weight, *small
        )
        return out

    rows = P("cfg", ("group", "seq", "head"), None)
    return jax.shard_map(
        local,
        mesh=mesh,
        in_specs=(
            rows, rows, rows, rows,
            P("head", None),
            P("cfg", "group", None),
            P(),
            P(("seq", "cfg"), None, "head"),
            P(("seq", "cfg"), None, "head"),
            P(("seq", "cfg"), "head", None),
            rows,
        ),
        out_specs=rows,
        check_vma=False,
    )
```
